256 devices in a mesh: blk: 8 (over y, core), wide: 8 (over z), dp: 4 (over x).
Axes of the slice: x: 4, y: 4, z: 8, core: 2. Of those that a mesh axis runs over, the one named last changes fastest.
Arguments:
- token_ids: int32 [32768], P(('dp', 'blk', 'wide')), parts along dimension 0, may hold values from 0 to 5
- embedding: float32 [6, 1536], replicated, may hold values from -3 to 3
- queries: bfloat16 [32768, 768], P(('dp', 'blk', 'wide')), parts along dimension 0, may hold values from -12 to 12
- key_rows: bfloat16 [32768, 768], P(('dp', 'blk', 'wide')), parts along dimension 0, may hold values from -6 to 6
- value_rows: bfloat16 [32768, 768], P(('dp', 'blk', 'wide')), parts along dimension 0, may hold values from -6 to 6
- head_mixer: bfloat16 [768, 1536], replicated, may hold values from -0.21875 to 0.21875
- expand_weight: bfloat16 [1536, 3072], P(None, 'wide'), may hold values from -0.15625 to 0.15625
- reduce_weight: bfloat16 [3072, 1536], P('wide'), may hold values from -0.109375 to 0.109375
- cotangent: bfloat16 [32768, 1536], P(('dp', 'blk', 'wide')), parts along dimension 0, may hold values from -0.29882812 to 0.29882812
Outputs:
- restored: bfloat16 [32768, 1536], P(('dp', 'blk', 'wide')), parts along dimension 0
- expand_grad: float32 [6144, 3072], P(('dp', 'blk'), 'wide'), parts along dimension 0
- reduce_grad: float32 [12288, 1536], P(('dp', 'wide'), 'blk'), parts along dimension 0
The draws below stay inside these ranges and needn't reach their ends.
There are 4 independent parts, one for each index of `dp`. The reference program is written for one: setup_inputs(seed, part) draws one part's arguments, and reference() takes and returns one part's arrays. A program takes and returns all parts, laid end to end along the dimension named above; an argument that names none is the same for every part. Nothing has to cross between parts.
All inputs are finite; a program needn't handle non-finite values.
Results may differ from the reference program's by a relative error of at most 0.018.
Values may be sent and summed in bfloat16 or wider, within the bound.
A program may use at most 128 MiB of HBM per device.

```python
import jax
import jax.numpy as jnp
from jax import lax

D = 1536
FINE_HEADS = 6
HEAD = 128
FF = 3072
VOCAB = 6
POOL = 8
QKV = 768
LENGTH = 8192


def draw_pair(key):
    array_shape = (LENGTH, QKV)
    query_base = jnp.clip(3.0 * jax.random.normal(jax.random.fold_in(key, 101), array_shape, jnp.float32), -12.0, 12.0)
    key_base = jnp.clip(jax.random.normal(jax.random.fold_in(key, 102), array_shape, jnp.float32), -5.5, 5.5)
    return (query_base, key_base)


def draw_queries(key, part):
    return draw_pair(key)[0].astype(jnp.bfloat16)


def draw_key_rows(key, part):
    return draw_pair(key)[1].astype(jnp.bfloat16)


def set_ends(values, own_key, smallest, high):
    spot = [jax.random.randint(jax.random.fold_in(own_key, axis), (), 0, length) for axis, length in enumerate(values.shape)]
    main_axis = values.shape.index(max(values.shape))
    neighbour = spot[:main_axis] + [(spot[main_axis] + 1) % values.shape[main_axis]] + spot[main_axis + 1:]
    return values.at[tuple(spot)].set(smallest).at[tuple(neighbour)].set(high)


def steps_of(rng, shape, shards, least, top_value):
    gain, own = 1.0, jax.random.fold_in(rng, 6)
    for position, blocks in shards:
        draws = jnp.exp(jax.random.uniform(jax.random.fold_in(own, position), (blocks,), jnp.float32, least / len(shards), top_value / len(shards)))
        gain = gain * jnp.repeat(draws, shape[position] // blocks).reshape([-1 if axis == position else 1 for axis in range(len(shape))])
    return gain


def scatter_about(stream_key, shape, spread, reach, cuts=(), held_as=jnp.bfloat16):
    values = jax.random.normal(stream_key, shape, jnp.float32) * spread
    if len(cuts) > 0:
        values = steps_of(stream_key, shape, cuts, -0.22, 0.18) * values
    return jnp.clip(values, min=-reach, max=reach).astype(held_as)


def setup_inputs(seed: int = 0, part: int = 0) -> dict:
    streams_of = jax.random.split(jax.random.key(seed), 10)
    part_keys = jax.random.split(jax.random.fold_in(streams_of[9], part), 10)
    token_ids = set_ends(jax.random.randint(part_keys[0], (LENGTH,), 0, VOCAB), jax.random.fold_in(part_keys[0], 1), 0, VOCAB - 1).astype(jnp.int32)
    embedding = scatter_about(streams_of[1], (VOCAB, D), 0.5, 3.0, (), jnp.float32)
    queries = draw_queries(jax.random.fold_in(jax.random.fold_in(streams_of[9], part), 71), part)
    key_rows = draw_key_rows(jax.random.fold_in(jax.random.fold_in(streams_of[9], part), 71), part)
    value_rows = scatter_about(part_keys[4], (LENGTH, QKV), 1.0, 6.0, ((0, 64),))
    head_mixer = scatter_about(streams_of[5], (QKV, D), QKV ** -0.5, 0.21875)
    expand_weight = scatter_about(streams_of[6], (D, FF), D ** -0.5, 0.15625, ((1, 8),))
    reduce_weight = scatter_about(streams_of[7], (FF, D), FF ** -0.5, 0.109375, ((0, 8),))
    cotangent = scatter_about(part_keys[8], (LENGTH, D), 0.05, 0.29882812, ((0, 64),))
    return {"token_ids": token_ids, "embedding": embedding, "queries": queries, "key_rows": key_rows, "value_rows": value_rows, "head_mixer": head_mixer, "expand_weight": expand_weight, "reduce_weight": reduce_weight, "cotangent": cotangent}


def reference(token_ids, embedding, queries, key_rows, value_rows, head_mixer, expand_weight, reduce_weight, cotangent):
    length = token_ids.shape[0]
    onehot = (token_ids[:, None] == jnp.arange(VOCAB, dtype=jnp.int32)[None, :]).astype(jnp.float32)
    embedded = jnp.dot(onehot, embedding, precision=lax.Precision.HIGHEST, preferred_element_type=jnp.float32)
    block_rows = 512 if length % 512 == 0 else length
    key_heads = key_rows.astype(jnp.float32).reshape(length, FINE_HEADS, HEAD)
    value_heads = value_rows.astype(jnp.float32).reshape(length, FINE_HEADS, HEAD)
    positions = jnp.arange(length, dtype=jnp.int32)

    def attend(packed):
        query_block, first_row = packed
        query_heads = query_block.astype(jnp.float32).reshape(block_rows, FINE_HEADS, HEAD)
        scores = jnp.einsum('rhd,khd->hrk', query_heads, key_heads) * HEAD ** (-0.5)
        query_position = first_row + jnp.arange(block_rows, dtype=jnp.int32)
        allowed = (positions[None, :] <= query_position[:, None])[None]
        scores = jnp.where(allowed, scores, -1e+30)
        row_max = scores.max(-1, keepdims=True)
        weights = jnp.where(allowed, jnp.exp(scores - row_max), 0.0)
        totals = weights.sum(-1)
        summed = jnp.einsum('hrk,khd->hrd', weights.astype(jnp.bfloat16).astype(jnp.float32), value_heads)
        result = summed / totals[..., None]
        return result.transpose(1, 0, 2).reshape(block_rows, QKV).astype(jnp.bfloat16)
    starts = jnp.arange(0, length, block_rows, dtype=jnp.int32)
    attended = lax.map(attend, (queries.reshape(-1, block_rows, QKV), starts)).reshape(length, QKV)
    stream = embedded + jnp.dot(attended, head_mixer, preferred_element_type=jnp.float32)
    shifted = jnp.concatenate([jnp.zeros((1, D), jnp.float32), stream[:-1]], 0)
    pooled = shifted.reshape(-1, POOL, D).mean(axis=1).astype(jnp.bfloat16)
    pooled_float = pooled.astype(jnp.float32)
    normed = (pooled_float * lax.rsqrt(lax.optimization_barrier(jnp.mean(pooled_float * pooled_float, -1, keepdims=True)) + 1e-06)).astype(jnp.bfloat16)
    expanded = jnp.dot(normed, expand_weight, preferred_element_type=jnp.float32)
    activated = jax.nn.gelu(expanded).astype(jnp.bfloat16)
    middle = pooled_float + jnp.dot(activated, reduce_weight, preferred_element_type=jnp.float32)
    before = jnp.concatenate([jnp.zeros((1, D), jnp.float32), middle[:-1]], 0)
    steps_index = jnp.arange(POOL, dtype=jnp.float32)
    after_weights = (steps_index + 1.0) / POOL
    before_weights = (POOL - 1.0 - steps_index) / POOL
    upsampled = (middle[:, None, :] * after_weights[None, :, None] + before[:, None, :] * before_weights[None, :, None]).reshape(length, D)
    restored = (stream + upsampled).astype(jnp.bfloat16)
    grad_rows = cotangent.astype(jnp.float32).reshape(-1, POOL, D)
    own_part = jnp.einsum('sid,i->sd', grad_rows, after_weights)
    later_part = jnp.einsum('sid,i->sd', grad_rows, before_weights)
    middle_grad = (own_part + jnp.concatenate([later_part[1:], jnp.zeros((1, D), jnp.float32)], 0)).astype(jnp.bfloat16)
    act_grad = jnp.dot(middle_grad, reduce_weight.T, preferred_element_type=jnp.float32)
    pre_grad = jax.vjp(jax.nn.gelu, expanded)[1](act_grad)[0].astype(jnp.bfloat16)
    expand_grad = jnp.dot(normed.T, pre_grad, preferred_element_type=jnp.float32)
    reduce_grad = jnp.dot(activated.T, middle_grad, preferred_element_type=jnp.float32)
    return (restored, expand_grad, reduce_grad)
```

```python
import jax
import jax.numpy as jnp
from jax import lax
from jax.experimental import pallas as pl
from jax.experimental.pallas import tpu as pltpu
from jax.sharding import PartitionSpec as P

FINE_HEADS = 6
HEAD = 128
VOCAB = 6
POOL = 8


def side_by_side(arrays, axis, dim, along):
    widths = [a.shape[along] for a in arrays]
    both = jnp.concatenate(arrays, axis=along)
    result = lax.all_gather(both, axis, axis=dim, tiled=True)
    return tuple(jnp.split(result, [sum(widths[:k]) for k in range(1, len(widths))], axis=along))


def from_behind(array, axis, by):
    size = lax.axis_size(axis)
    pairs = [(i, i + by) for i in range(size) if 0 <= i + by < size]
    return lax.ppermute(array, axis, pairs)


def in_order(blocks, dim):
    shape = list(blocks.shape[1:])
    shape[dim] *= blocks.shape[0]
    return jnp.moveaxis(blocks, 0, dim).reshape(shape)


def copy_for_each(array, axis):
    copies = jnp.broadcast_to(array, (lax.axis_size(axis), *array.shape))
    return lax.all_to_all(copies, axis, split_axis=0, concat_axis=0, tiled=True)


def gather_directly(array, axis, dim):
    return in_order(copy_for_each(array, axis), dim)


def in_blocks(array, dim, size):
    before, after = (array.shape[:dim], array.shape[dim + 1 :])
    return jnp.moveaxis(array.reshape(*before, size, -1, *after), dim, 0)


def sum_at_owner(array, axis, dim):
    blocks = in_blocks(array, dim, lax.axis_size(axis))
    arrived = lax.all_to_all(blocks, axis, split_axis=0, concat_axis=0, tiled=True)
    return arrived.astype(jnp.float32).sum(axis=0)


MESH = pl.DeviceIdType.MESH
ROUNDS = 8
SCALE = HEAD ** (-0.5) * 1.4426950408889634
MASKED = -2e38
EMPTY = -1e30


def offset_of(r):
    return (r + 1) // 2 * (2 * (r % 2) - 1)


def landed(ref, sem):
    pltpu.make_async_copy(ref, ref, sem).wait()


def attention_kernel(
    q_ref,
    k_ref,
    v_ref,
    out_ref,
    qbuf,
    kvbuf,
    acc,
    maxima,
    obuf,
    abuf,
    q_send,
    kv_send,
    own_send,
    relay_send,
    opp_send,
    o_send,
    q_recv,
    kv_recv,
    o_recv,
):
    b = lax.axis_index("blk")
    z = lax.axis_index("wide")
    sibling = b + 1 - 2 * lax.rem(b, 2)
    up = lax.rem(b + 2, 8)
    down = lax.rem(b + 6, 8)
    across = lax.rem(b + 4, 8)

    barrier = pltpu.get_barrier_semaphore()

    @pl.loop(0, 64)
    def _(i):
        ib, iz = i // 8, lax.rem(i, 8)

        @pl.when(i != b * 8 + z)
        def _():
            pl.semaphore_signal(
                barrier, inc=1, device_id={"blk": ib, "wide": iz}, device_id_type=MESH
            )

    acc[...] = jnp.zeros_like(acc)
    maxima[...] = jnp.full_like(maxima, EMPTY)
    pl.semaphore_wait(barrier, 63)

    def head_columns(h):
        return pl.ds(pl.multiple_of(h * HEAD, HEAD), HEAD)

    def kv_copies(r, h):
        copies = []
        for n, ref in enumerate((k_ref, v_ref)):
            copies.append(
                pltpu.make_async_remote_copy(
                    src_ref=ref.at[:, head_columns(h)],
                    dst_ref=kvbuf.at[r, n, b],
                    send_sem=kv_send.at[r, n],
                    recv_sem=kv_recv.at[r, b],
                    device_id={"blk": b, "wide": h},
                    device_id_type=MESH,
                )
            )
        return copies

    def q_copy(h):
        return pltpu.make_async_remote_copy(
            src_ref=q_ref.at[:, head_columns(h)],
            dst_ref=qbuf.at[b],
            send_sem=q_send.at[h],
            recv_sem=q_recv.at[b],
            device_id={"blk": z, "wide": h},
            device_id_type=MESH,
        )

    def q_local():
        return pltpu.make_async_copy(q_ref.at[:, head_columns(z)], qbuf.at[b], q_recv.at[b])

    def is_self(h):
        return jnp.logical_and(z == b, h == z)

    @pl.when(z < FINE_HEADS)
    def _():
        for n, ref in enumerate((k_ref, v_ref)):
            pltpu.make_async_copy(
                ref.at[:, head_columns(z)], kvbuf.at[0, n, b], kv_recv.at[0, b]
            ).start()

    def send_round(r):
        h = lax.rem(z - offset_of(r) + 8, 8)

        @pl.when(h < FINE_HEADS)
        def _():
            for copy in kv_copies(r, h):
                copy.start()

    def wait_round(r):
        h = lax.rem(z - offset_of(r) + 8, 8)

        @pl.when(h < FINE_HEADS)
        def _():
            for copy in kv_copies(r, h):
                copy.wait_send()

    send_round(1)
    send_round(2)

    @pl.loop(0, FINE_HEADS)
    def _(h):
        @pl.when(is_self(h))
        def _():
            q_local().start()

        @pl.when(jnp.logical_not(is_self(h)))
        def _():
            q_copy(h).start()

    for r in range(3, ROUNDS):
        send_round(r)

    def piece(r, blk):
        return kvbuf.at[r, :, blk]

    def pass_on(src, sem, recv, blk):
        return pltpu.make_async_remote_copy(
            src_ref=src,
            dst_ref=src,
            send_sem=sem,
            recv_sem=recv,
            device_id={"blk": blk, "wide": z},
            device_id_type=MESH,
        )

    def own_copies(r):
        recv = kv_recv.at[r, b]
        return [
            pass_on(piece(r, b), own_send.at[r, n], recv, blk)
            for n, blk in enumerate((up, down, sibling))
        ]

    def relay_copies(r):
        return [
            [
                pass_on(kvbuf.at[r, 0, down], relay_send.at[r, 0], kv_recv.at[r, down], up),
                pass_on(piece(r, down), relay_send.at[r, 1], kv_recv.at[r, down], sibling),
            ],
            [
                pass_on(kvbuf.at[r, 1, up], relay_send.at[r, 2], kv_recv.at[r, up], down),
                pass_on(piece(r, up), relay_send.at[r, 3], kv_recv.at[r, up], sibling),
            ],
        ]

    def opp_copy(r):
        return pass_on(piece(r, across), opp_send.at[r], kv_recv.at[r, across], sibling)

    def compute(r):
        source = lax.rem(z + offset_of(r) + 8, 8)
        rows = lax.broadcasted_iota(jnp.int32, (HEAD, HEAD), 0)
        cols = lax.broadcasted_iota(jnp.int32, (HEAD, HEAD), 1)
        allowed = cols + (source - b) * HEAD <= rows
        for n in range(8):
            keys = kvbuf[r, 0, : n + 1].reshape((n + 1) * HEAD, HEAD)
            values = kvbuf[r, 1, : n + 1].reshape((n + 1) * HEAD, HEAD)
            scores = lax.dot_general(
                qbuf[n], keys, (((1,), (1,)), ((), ())), preferred_element_type=jnp.float32
            )
            last = jnp.where(allowed, scores[:, n * HEAD :], MASKED)
            if n:
                scores = jnp.concatenate([scores[:, : n * HEAD], last], 1)
            else:
                scores = last
            before = maxima[n]
            highest = jnp.maximum(before, scores.max(-1, keepdims=True) * SCALE)
            weights = jnp.exp2(scores * SCALE - jnp.concatenate([highest] * (n + 1), 1))
            factor = jnp.exp2(before - highest)
            extended = jnp.concatenate([values, jnp.ones_like(values)], 1)
            summed = jnp.dot(
                weights.astype(jnp.bfloat16), extended, preferred_element_type=jnp.float32
            )
            acc[n] = acc[n] * jnp.concatenate([factor, factor], 1) + summed
            maxima[n] = highest

    def o_copy(n):
        return pltpu.make_async_remote_copy(
            src_ref=obuf.at[n],
            dst_ref=abuf.at[:, head_columns(z)],
            send_sem=o_send.at[n],
            recv_sem=o_recv,
            device_id={"blk": n, "wide": b},
            device_id_type=MESH,
        )

    def o_local(n):
        return pltpu.make_async_copy(obuf.at[n], abuf.at[:, head_columns(z)], o_recv)

    @pl.when(z < FINE_HEADS)
    def _():
        @pl.loop(0, ROUNDS + 3)
        def _(i):
            @pl.when(jnp.logical_and(i >= 1, i < ROUNDS + 1))
            def _():
                first, second = relay_copies(i - 1)
                landed(piece(i - 1, down), kv_recv.at[i - 1, down])
                for copy in first:
                    copy.start()
                landed(piece(i - 1, up), kv_recv.at[i - 1, up])
                for copy in second:
                    copy.start()

            @pl.when(i < ROUNDS)
            def _():
                landed(piece(i, b), kv_recv.at[i, b])
                for copy in own_copies(i):
                    copy.start()

            @pl.when(jnp.logical_and(i >= 2, i < ROUNDS + 2))
            def _():
                landed(piece(i - 2, across), kv_recv.at[i - 2, across])
                opp_copy(i - 2).start()

            @pl.when(i == 3)
            def _():
                for n in range(8):
                    landed(qbuf.at[n], q_recv.at[n])

            @pl.when(i >= 3)
            def _():
                for n in range(4):
                    other = lax.rem(sibling + 2 * n, 8)
                    landed(piece(i - 3, other), kv_recv.at[i - 3, other])
                compute(i - 3)

        for n in range(8):
            total = acc[n]
            obuf[n] = (total[:, :HEAD] / total[:, HEAD:]).astype(jnp.bfloat16)
            here = jnp.logical_and(n == b, z == b)

            @pl.when(here)
            def _():
                o_local(n).start()

            @pl.when(jnp.logical_not(here))
            def _():
                o_copy(n).start()

        @pl.loop(0, ROUNDS)
        def _(r):
            for copy in own_copies(r):
                copy.wait_send()
            for pair in relay_copies(r):
                for copy in pair:
                    copy.wait_send()
            opp_copy(r).wait_send()

        for n in range(8):

            @pl.when(jnp.logical_not(jnp.logical_and(n == b, z == b)))
            def _():
                o_copy(n).wait_send()

    for r in range(1, ROUNDS):
        wait_round(r)

    @pl.loop(0, FINE_HEADS)
    def _(h):
        @pl.when(jnp.logical_not(is_self(h)))
        def _():
            q_copy(h).wait_send()

    landed(abuf, o_recv)
    out_ref[...] = abuf[...]


def attention(queries, key_rows, value_rows):
    rows, width = queries.shape
    vmem = pl.BlockSpec(memory_space=pltpu.VMEM)
    dma = pltpu.SemaphoreType.DMA
    return pl.pallas_call(
        attention_kernel,
        name="attention",
        out_shape=jax.ShapeDtypeStruct((rows, width), jnp.bfloat16),
        in_specs=[vmem] * 3,
        out_specs=vmem,
        scratch_shapes=[
            pltpu.VMEM((8, rows, HEAD), jnp.bfloat16),
            pltpu.VMEM((ROUNDS, 2, 8, rows, HEAD), jnp.bfloat16),
            pltpu.VMEM((8, rows, 2 * HEAD), jnp.float32),
            pltpu.VMEM((8, rows, HEAD), jnp.float32),
            pltpu.VMEM((8, rows, HEAD), jnp.bfloat16),
            pltpu.VMEM((rows, width), jnp.bfloat16),
            dma((FINE_HEADS,)),
            dma((ROUNDS, 2)),
            dma((ROUNDS, 3)),
            dma((ROUNDS, 4)),
            dma((ROUNDS,)),
            dma((8,)),
            dma((8,)),
            dma((ROUNDS, 8)),
            dma,
        ],
        compiler_params=pltpu.CompilerParams(collective_id=0, has_side_effects=True),
    )(queries, key_rows, value_rows)


def local(
    token_ids,
    embedding,
    queries,
    key_rows,
    value_rows,
    head_mixer,
    expand_weight,
    reduce_weight,
    cotangent,
):
    attended = attention(queries, key_rows, value_rows)
    onehot = (token_ids[:, None] == jnp.arange(VOCAB, dtype=jnp.int32)[None, :]).astype(jnp.float32)
    stream = jnp.dot(
        onehot, embedding, precision=lax.Precision.HIGHEST, preferred_element_type=jnp.float32
    )
    stream = stream + jnp.dot(attended, head_mixer, preferred_element_type=jnp.float32)
    carried = from_behind(stream[-1:], ("blk", "wide"), 1)
    shifted = jnp.concatenate([carried, stream[:-1]], 0)
    pooled = shifted.reshape(-1, POOL, stream.shape[1]).mean(axis=1).astype(jnp.bfloat16)
    pooled_wide = gather_directly(pooled, "wide", 0)
    pooled_float = pooled_wide.astype(jnp.float32)
    normed = (
        pooled_float * lax.rsqrt(jnp.mean(pooled_float * pooled_float, -1, keepdims=True) + 1e-06)
    ).astype(jnp.bfloat16)
    expanded = jnp.dot(normed, expand_weight, preferred_element_type=jnp.float32)
    activated = jax.nn.gelu(expanded).astype(jnp.bfloat16)
    middle = pooled.astype(jnp.float32) + sum_at_owner(
        jnp.dot(activated, reduce_weight, preferred_element_type=jnp.float32).astype(jnp.bfloat16),
        "wide",
        0,
    )
    earlier = from_behind(middle[-1:], ("blk", "wide"), 1)
    before = jnp.concatenate([earlier, middle[:-1]], 0)
    steps_index = jnp.arange(POOL, dtype=jnp.float32)
    after_weights = (steps_index + 1.0) / POOL
    before_weights = (POOL - 1.0 - steps_index) / POOL
    upsampled = (
        middle[:, None, :] * after_weights[None, :, None]
        + before[:, None, :] * before_weights[None, :, None]
    ).reshape(stream.shape)
    restored = (stream + upsampled).astype(jnp.bfloat16)
    grad_rows = cotangent.astype(jnp.float32).reshape(-1, POOL, stream.shape[1])
    own_part = jnp.einsum("sid,i->sd", grad_rows, after_weights)
    later_part = jnp.einsum("sid,i->sd", grad_rows, before_weights)
    following = from_behind(later_part[:1], ("blk", "wide"), -1)
    middle_grad = (own_part + jnp.concatenate([later_part[1:], following], 0)).astype(jnp.bfloat16)
    grad_wide = gather_directly(middle_grad, "wide", 0)
    act_grad = lax.dot_general(
        grad_wide, reduce_weight, (((1,), (1,)), ((), ())), preferred_element_type=jnp.float32
    )
    pre_grad = jax.vjp(jax.nn.gelu, expanded)[1](act_grad)[0].astype(jnp.bfloat16)
    normed_cols, grad_cols = (
        lax.all_to_all(normed, "blk", split_axis=1, concat_axis=0, tiled=True),
        lax.all_to_all(grad_wide, "blk", split_axis=1, concat_axis=0, tiled=True),
    )
    pre_all, act_all = side_by_side((pre_grad, activated), "blk", 0, 1)
    expand_grad = jnp.einsum("gi,gj->ij", normed_cols, pre_all, preferred_element_type=jnp.float32)
    reduce_grad = jnp.einsum("gi,gj->ij", act_all, grad_cols, preferred_element_type=jnp.float32)
    return (restored, expand_grad, reduce_grad)


def solution(mesh):
    return jax.shard_map(
        local,
        mesh=mesh,
        in_specs=(
            P(("dp", "blk", "wide")),
            P(),
            P(("dp", "blk", "wide"), None),
            P(("dp", "blk", "wide"), None),
            P(("dp", "blk", "wide"), None),
            P(),
            P(None, "wide"),
            P("wide", None),
            P(("dp", "blk", "wide"), None),
        ),
        out_specs=(
            P(("dp", "blk", "wide"), None),
            P(("dp", "blk"), "wide"),
            P(("dp", "wide"), "blk"),
        ),
        check_vma=False,
    )
```

```python
import jax
import jax.numpy as jnp
from jax import lax
from jax.experimental import pallas as pl
from jax.experimental.pallas import tpu as pltpu
from jax.sharding import PartitionSpec as P

FINE_HEADS = 6
HEAD = 128
VOCAB = 6


MESH = pl.DeviceIdType.MESH
ROUNDS = 8
RELAY, ACROSS, LAST = 2, 3, 4
SCALE = HEAD ** (-0.5) * 1.4426950408889634
MASKED = -2e38
EMPTY = -1e30


def offset_of(r):
    return (r + 1) // 2 * (2 * (r % 2) - 1)


def landed(ref, sem):
    pltpu.make_async_copy(ref, ref, sem).wait()


def attention_kernel(
    q_ref,
    k_ref,
    v_ref,
    out_ref,
    qbuf,
    kvbuf,
    acc,
    maxima,
    obuf,
    abuf,
    q_send,
    kv_send,
    own_send,
    relay_send,
    opp_send,
    o_send,
    q_recv,
    kv_recv,
    o_recv,
):
    b = lax.axis_index("blk")
    z = lax.axis_index("wide")
    sibling = b + 1 - 2 * lax.rem(b, 2)
    up = lax.rem(b + 2, 8)
    down = lax.rem(b + 6, 8)
    across = lax.rem(b + 4, 8)

    home = lax.rem(b + 3 * z, 8)

    def holder(wide, h):
        return lax.rem(wide + 5 * h, 8)

    barrier = pltpu.get_barrier_semaphore()

    def greet(blk, wide):
        pl.semaphore_signal(
            barrier, inc=1, device_id={"blk": blk, "wide": wide}, device_id_type=MESH
        )

    holds_head = z < FINE_HEADS
    diagonal = z == home

    @pl.loop(1, 8)
    def _(j):
        greet(b, lax.rem(z + j, 8))

    @pl.loop(0, FINE_HEADS)
    def _(h):
        @pl.when(jnp.logical_not(jnp.logical_and(diagonal, h == z)))
        def _():
            greet(holder(z, h), h)

    @pl.when(holds_head)
    def _():
        @pl.loop(0, 8)
        def _(n):
            @pl.when(jnp.logical_not(jnp.logical_and(diagonal, n == b)))
            def _():
                greet(n, home)

        for blk in (up, down, sibling):
            greet(blk, z)

    acc[...] = jnp.zeros_like(acc)
    maxima[...] = jnp.full_like(maxima, EMPTY)

    @pl.when(holds_head)
    def _():
        pl.semaphore_wait(barrier, 24 - 2 * diagonal.astype(jnp.int32))

    @pl.when(jnp.logical_not(holds_head))
    def _():
        pl.semaphore_wait(barrier, 13)

    def head_columns(h):
        return pl.ds(pl.multiple_of(h * HEAD, HEAD), HEAD)

    def kv_copies(r, h):
        copies = []
        for n, ref in enumerate((k_ref, v_ref)):
            copies.append(
                pltpu.make_async_remote_copy(
                    src_ref=ref.at[:, head_columns(h)],
                    dst_ref=kvbuf.at[r, n, b],
                    send_sem=kv_send.at[r, n],
                    recv_sem=kv_recv.at[r, b],
                    device_id={"blk": b, "wide": h},
                    device_id_type=MESH,
                )
            )
        return copies

    def q_copy(h):
        return pltpu.make_async_remote_copy(
            src_ref=q_ref.at[:, head_columns(h)],
            dst_ref=qbuf.at[b],
            send_sem=q_send.at[h],
            recv_sem=q_recv.at[b],
            device_id={"blk": holder(z, h), "wide": h},
            device_id_type=MESH,
        )

    def q_local():
        return pltpu.make_async_copy(q_ref.at[:, head_columns(z)], qbuf.at[b], q_recv.at[b])

    def is_self(h):
        return jnp.logical_and(z == home, h == z)

    @pl.when(z < FINE_HEADS)
    def _():
        for n, ref in enumerate((k_ref, v_ref)):
            pltpu.make_async_copy(
                ref.at[:, head_columns(z)], kvbuf.at[0, n, b], kv_recv.at[0, b]
            ).start()

    def send_round(r):
        h = lax.rem(z - offset_of(r) + 8, 8)

        @pl.when(h < FINE_HEADS)
        def _():
            for copy in kv_copies(r, h):
                copy.start()

    def wait_round(r):
        h = lax.rem(z - offset_of(r) + 8, 8)

        @pl.when(h < FINE_HEADS)
        def _():
            for copy in kv_copies(r, h):
                copy.wait_send()

    send_round(1)
    send_round(2)

    @pl.loop(0, FINE_HEADS)
    def _(h):
        @pl.when(is_self(h))
        def _():
            q_local().start()

        @pl.when(jnp.logical_not(is_self(h)))
        def _():
            q_copy(h).start()

    for r in range(3, ROUNDS):
        send_round(r)

    def piece(r, blk):
        return kvbuf.at[r, :, blk]

    def pass_on(src, sem, recv, blk):
        return pltpu.make_async_remote_copy(
            src_ref=src,
            dst_ref=src,
            send_sem=sem,
            recv_sem=recv,
            device_id={"blk": blk, "wide": z},
            device_id_type=MESH,
        )

    def own_copies(r):
        recv = kv_recv.at[r, b]
        return [
            pass_on(piece(r, b), own_send.at[r, n], recv, blk)
            for n, blk in enumerate((up, down, sibling))
        ]

    def relay_copies(r):
        return [
            [
                pass_on(kvbuf.at[r, 0, down], relay_send.at[r, 0], kv_recv.at[r, down], up),
                pass_on(piece(r, down), relay_send.at[r, 1], kv_recv.at[r, down], sibling),
            ],
            [
                pass_on(kvbuf.at[r, 1, up], relay_send.at[r, 2], kv_recv.at[r, up], down),
                pass_on(piece(r, up), relay_send.at[r, 3], kv_recv.at[r, up], sibling),
            ],
        ]

    def opp_copy(r):
        return pass_on(piece(r, across), opp_send.at[r], kv_recv.at[r, across], sibling)

    def compute(r):
        source = lax.rem(z + offset_of(r) + 8, 8)
        rows = lax.broadcasted_iota(jnp.int32, (HEAD, HEAD), 0)
        cols = lax.broadcasted_iota(jnp.int32, (HEAD, HEAD), 1)
        allowed = cols + (source - home) * HEAD <= rows
        for n in range(8):
            keys = kvbuf[r, 0, : n + 1].reshape((n + 1) * HEAD, HEAD)
            values = kvbuf[r, 1, : n + 1].reshape((n + 1) * HEAD, HEAD)
            scores = lax.dot_general(
                qbuf[n], keys, (((1,), (1,)), ((), ())), preferred_element_type=jnp.float32
            )
            last = jnp.where(allowed, scores[:, n * HEAD :], MASKED)
            if n:
                scores = jnp.concatenate([scores[:, : n * HEAD], last], 1)
            else:
                scores = last
            before = maxima[n]
            highest = jnp.maximum(before, scores.max(-1, keepdims=True) * SCALE)
            weights = jnp.exp2(scores * SCALE - jnp.concatenate([highest] * (n + 1), 1))
            factor = jnp.exp2(before - highest)
            extended = jnp.concatenate([values, jnp.ones_like(values)], 1)
            summed = jnp.dot(
                weights.astype(jnp.bfloat16), extended, preferred_element_type=jnp.float32
            )
            acc[n] = acc[n] * jnp.concatenate([factor, factor], 1) + summed
            maxima[n] = highest

    def o_copy(n):
        return pltpu.make_async_remote_copy(
            src_ref=obuf.at[n],
            dst_ref=abuf.at[:, head_columns(z)],
            send_sem=o_send.at[n],
            recv_sem=o_recv,
            device_id={"blk": n, "wide": home},
            device_id_type=MESH,
        )

    def o_local(n):
        return pltpu.make_async_copy(obuf.at[n], abuf.at[:, head_columns(z)], o_recv)

    @pl.when(z < FINE_HEADS)
    def _():
        @pl.loop(0, ROUNDS + LAST)
        def _(i):
            def stage(late):
                return jnp.logical_and(i >= late, i < ROUNDS + late)

            @pl.when(i < ROUNDS)
            def _():
                landed(piece(i, b), kv_recv.at[i, b])
                for copy in own_copies(i):
                    copy.start()

            @pl.when(stage(RELAY))
            def _():
                r = i - RELAY
                first, second = relay_copies(r)
                landed(piece(r, down), kv_recv.at[r, down])
                for copy in first:
                    copy.start()
                landed(piece(r, up), kv_recv.at[r, up])
                for copy in second:
                    copy.start()

            @pl.when(stage(ACROSS))
            def _():
                r = i - ACROSS
                landed(piece(r, across), kv_recv.at[r, across])
                opp_copy(r).start()

            @pl.when(i == LAST)
            def _():
                for n in range(8):
                    landed(qbuf.at[n], q_recv.at[n])

            @pl.when(i >= LAST)
            def _():
                r = i - LAST
                for n in range(4):
                    other = lax.rem(sibling + 2 * n, 8)
                    landed(piece(r, other), kv_recv.at[r, other])
                compute(r)

        for n in range(8):
            total = acc[n]
            obuf[n] = (total[:, :HEAD] / total[:, HEAD:]).astype(jnp.bfloat16)
            here = jnp.logical_and(n == b, z == home)

            @pl.when(here)
            def _():
                o_local(n).start()

            @pl.when(jnp.logical_not(here))
            def _():
                o_copy(n).start()

        @pl.loop(0, ROUNDS)
        def _(r):
            for copy in own_copies(r):
                copy.wait_send()
            for pair in relay_copies(r):
                for copy in pair:
                    copy.wait_send()
            opp_copy(r).wait_send()

        for n in range(8):

            @pl.when(jnp.logical_not(jnp.logical_and(n == b, z == home)))
            def _():
                o_copy(n).wait_send()

    for r in range(1, ROUNDS):
        wait_round(r)

    @pl.loop(0, FINE_HEADS)
    def _(h):
        @pl.when(jnp.logical_not(is_self(h)))
        def _():
            q_copy(h).wait_send()

    landed(abuf, o_recv)
    out_ref[...] = abuf[...]


def attention(queries, key_rows, value_rows):
    rows, width = queries.shape
    vmem = pl.BlockSpec(memory_space=pltpu.VMEM)
    dma = pltpu.SemaphoreType.DMA
    return pl.pallas_call(
        attention_kernel,
        name="attention",
        out_shape=jax.ShapeDtypeStruct((rows, width), jnp.bfloat16),
        in_specs=[vmem] * 3,
        out_specs=vmem,
        scratch_shapes=[
            pltpu.VMEM((8, rows, HEAD), jnp.bfloat16),
            pltpu.VMEM((ROUNDS, 2, 8, rows, HEAD), jnp.bfloat16),
            pltpu.VMEM((8, rows, 2 * HEAD), jnp.float32),
            pltpu.VMEM((8, rows, HEAD), jnp.float32),
            pltpu.VMEM((8, rows, HEAD), jnp.bfloat16),
            pltpu.VMEM((rows, width), jnp.bfloat16),
            dma((FINE_HEADS,)),
            dma((ROUNDS, 2)),
            dma((ROUNDS, 3)),
            dma((ROUNDS, 4)),
            dma((ROUNDS,)),
            dma((8,)),
            dma((8,)),
            dma((ROUNDS, 8)),
            dma,
        ],
        compiler_params=pltpu.CompilerParams(collective_id=0, has_side_effects=True),
    )(queries, key_rows, value_rows)


def gelu_parts(x):
    root = 0.7978845608028654
    inner = jnp.tanh(root * (x + 0.044715 * x * x * x))
    slope = 0.5 * (1.0 + inner) + 0.5 * x * (1.0 - inner * inner) * root * (
        1.0 + 3 * 0.044715 * x * x
    )
    return 0.5 * x * (1.0 + inner), slope


def middle_kernel(
    tok_ref,
    emb_ref,
    att_ref,
    mixer_ref,
    w1_ref,
    w2_ref,
    cot_ref,
    restored_ref,
    expand_ref,
    reduce_ref,
    sbuf,
    lbuf,
    mbuf,
    row_out,
    row_in,
    pw,
    gw,
    nbuf,
    pbuf,
    rsb,
    ab,
    nwin,
    gwin,
    row_send,
    row_recv,
    pw_send,
    gw_send,
    rs_send,
    ab_send,
    sib_send,
    nwin_send,
    gwin_send,
    pw_recv,
    gw_recv,
    rs_recv,
    ab_recv,
    nwin_recv,
    gwin_recv,
):
    b = lax.axis_index("blk")
    z = lax.axis_index("wide")
    place = b * 8 + z
    sibling = b + 1 - 2 * lax.rem(b, 2)
    first, last = place == 0, place == 63
    not_first, not_last = place > 0, place < 63
    following = {"blk": lax.rem(b + (z + 1) // 8, 8), "wide": lax.rem(z + 1, 8)}
    preceding = {"blk": lax.rem(b + 8 - (8 - z) // 8, 8), "wide": lax.rem(z + 7, 8)}

    barrier = pltpu.get_barrier_semaphore()

    def greet(where):
        pl.semaphore_signal(barrier, inc=1, device_id=where, device_id_type=MESH)

    @pl.loop(1, 8)
    def _(j):
        greet({"blk": b, "wide": lax.rem(z + j, 8)})
        greet({"blk": lax.rem(b + j, 8), "wide": z})

    @pl.when(not_last)
    def _():
        greet(following)

    @pl.when(not_first)
    def _():
        greet(preceding)

    def remote(src, dst, send, recv, where):
        return pltpu.make_async_remote_copy(
            src_ref=src,
            dst_ref=dst,
            send_sem=send,
            recv_sem=recv,
            device_id=where,
            device_id_type=MESH,
        )

    eight = lax.broadcasted_iota(jnp.int32, (8, 1536), 0)

    def at_row(n, row):
        return jnp.where(eight == n, jnp.broadcast_to(row, (8, 1536)), 0.0)

    def row_copy(n, where):
        return remote(row_out.at[n], row_in.at[n], row_send.at[n], row_recv.at[n], where)

    short = lax.broadcasted_iota(jnp.int32, (16, 128), 0)
    inside = lax.broadcasted_iota(jnp.int32, (16, 128), 1) - 8 * short
    own = jnp.logical_and(inside >= 0, inside < 8)
    inside = inside.astype(jnp.float32)
    after = jnp.where(own, (inside + 1.0) / 8, 0.0).astype(jnp.bfloat16)
    before = jnp.where(own, (7.0 - inside) / 8, 0.0).astype(jnp.bfloat16)
    cot = cot_ref[...]
    later_part = jnp.dot(before, cot, preferred_element_type=jnp.float32)
    lbuf[:16] = later_part
    row_out[1] = later_part[:1]

    kind = lax.broadcasted_iota(jnp.int32, (VOCAB, 128), 0)
    onehot = (kind == tok_ref[...]).astype(jnp.float32)
    stream = lax.dot_general(
        onehot,
        emb_ref[...],
        (((0,), (0,)), ((), ())),
        precision=lax.Precision.HIGHEST,
        preferred_element_type=jnp.float32,
    )
    stream = stream + jnp.dot(att_ref[...], mixer_ref[...], preferred_element_type=jnp.float32)
    sbuf[8:] = stream
    row_out[0] = stream[127:]

    pl.semaphore_wait(
        barrier, 14 + not_first.astype(jnp.int32) + not_last.astype(jnp.int32)
    )

    @pl.when(not_last)
    def _():
        row_copy(0, following).start()

    @pl.when(not_first)
    def _():
        row_copy(1, preceding).start()

    own_part = jnp.dot(after, cot, preferred_element_type=jnp.float32)

    @pl.when(first)
    def _():
        row_in[0] = jnp.zeros((1, 1536), jnp.float32)
        row_in[2] = jnp.zeros((1, 1536), jnp.float32)

    @pl.when(last)
    def _():
        row_in[1] = jnp.zeros((1, 1536), jnp.float32)

    @pl.when(not_first)
    def _():
        landed(row_in.at[0], row_recv.at[0])

    sbuf[:8] = at_row(7, row_in[0])
    short = lax.broadcasted_iota(jnp.int32, (16, 136), 0)
    inside = lax.broadcasted_iota(jnp.int32, (16, 136), 1) - 8 * short
    pool = jnp.where(jnp.logical_and(inside >= 7, inside < 15), 0.125, 0.0)
    pooled = jnp.dot(
        pool, sbuf[...], precision=lax.Precision.HIGHEST, preferred_element_type=jnp.float32
    ).astype(jnp.bfloat16)
    mine = pl.ds(pl.multiple_of(z * 16, 16), 16)
    pw[mine, :] = pooled

    def wide_copy(buf, send, recv, j):
        where = {"blk": b, "wide": lax.rem(z + j, 8)}
        return remote(buf.at[mine], buf.at[mine], send.at[j - 1], recv, where)

    @pl.loop(1, 8)
    def _(j):
        wide_copy(pw, pw_send, pw_recv, j).start()

    @pl.when(not_last)
    def _():
        landed(row_in.at[1], row_recv.at[1])

    lbuf[16:] = at_row(0, row_in[1])
    middle_grad = (own_part + lbuf[1:17]).astype(jnp.bfloat16)
    gw[mine, :] = middle_grad

    @pl.loop(1, 8)
    def _(j):
        wide_copy(gw, gw_send, gw_recv, j).start()

    landed(pw.at[pl.ds(0, 112)], pw_recv)
    pooled_wide = pw[...].astype(jnp.float32)
    scale = lax.rsqrt(jnp.mean(pooled_wide * pooled_wide, -1, keepdims=True) + 1e-06)
    normed = (pooled_wide * scale).astype(jnp.bfloat16)
    nbuf[...] = normed
    expanded = jnp.dot(normed, w1_ref[...], preferred_element_type=jnp.float32)
    activated, slope = gelu_parts(expanded)
    activated = activated.astype(jnp.bfloat16)
    ab[b, :, :384] = activated
    pbuf[...] = jnp.dot(
        activated, w2_ref[...], preferred_element_type=jnp.float32
    ).astype(jnp.bfloat16)

    def sum_copy(j):
        to = lax.rem(z + j, 8)
        return remote(
            pbuf.at[pl.ds(pl.multiple_of(to * 16, 16), 16)],
            rsb.at[j - 1],
            rs_send.at[j - 1],
            rs_recv,
            {"blk": b, "wide": to},
        )

    @pl.loop(1, 8)
    def _(j):
        sum_copy(j).start()

    landed(gw.at[pl.ds(0, 112)], gw_recv)
    act_grad = lax.dot_general(
        gw[...], w2_ref[...], (((1,), (1,)), ((), ())), preferred_element_type=jnp.float32
    )
    ab[b, :, 384:] = (act_grad * slope).astype(jnp.bfloat16)

    def same_core(j):
        return remote(
            ab.at[b],
            ab.at[b],
            ab_send.at[j - 1],
            ab_recv.at[b],
            {"blk": lax.rem(b + 2 * j, 8), "wide": z},
        )

    def share(slot, n):
        return remote(
            ab.at[slot], ab.at[slot], sib_send.at[n], ab_recv.at[slot], {"blk": sibling, "wide": z}
        )

    def window(ref, to):
        return ref.at[:, pl.ds(pl.multiple_of(to * 192 // 128 * 128, 128), 256)]

    def window_copy(src, dst, send, recv, j):
        to = lax.rem(b + j, 8)
        return remote(
            window(src, to), dst.at[b], send.at[j - 1], recv, {"blk": to, "wide": z}
        )

    @pl.loop(1, 4)
    def _(j):
        same_core(j).start()

    share(b, 0).start()
    kept = [
        pltpu.make_async_copy(window(nbuf, b), nwin.at[b], nwin_send.at[7]),
        pltpu.make_async_copy(window(gw, b), gwin.at[b], gwin_send.at[7]),
    ]
    for copy in kept:
        copy.start()

    @pl.loop(1, 8)
    def _(j):
        window_copy(nbuf, nwin, nwin_send, nwin_recv, j).start()

    @pl.loop(1, 8)
    def _(j):
        window_copy(gw, gwin, gwin_send, gwin_recv, j).start()

    landed(rsb, rs_recv)
    middle = pw[mine, :].astype(jnp.float32) + pbuf[mine, :].astype(jnp.float32)
    for n in range(7):
        middle = middle + rsb[n].astype(jnp.float32)
    mbuf[8:] = middle
    row_out[2] = middle[15:]

    @pl.when(not_last)
    def _():
        row_copy(2, following).start()

    for j in range(1, 4):
        slot = lax.rem(b + 2 * j, 8)
        landed(ab.at[slot], ab_recv.at[slot])
        share(slot, j).start()

    @pl.when(not_first)
    def _():
        landed(row_in.at[2], row_recv.at[2])

    mbuf[:8] = at_row(7, row_in[2])
    steps = lax.broadcasted_iota(jnp.int32, (8, 1536), 0).astype(jnp.float32)
    ahead, behind = (steps + 1.0) / 8, (7.0 - steps) / 8
    for j in range(0, 16, 2):
        rows = [
            sbuf[8 * (n + 1) : 8 * (n + 2)]
            + mbuf[8 + n : 9 + n] * ahead
            + mbuf[7 + n : 8 + n] * behind
            for n in (j, j + 1)
        ]
        restored_ref[8 * j : 8 * (j + 2)] = jnp.concatenate(rows, 0).astype(jnp.bfloat16)

    for n in range(4):
        slot = lax.rem(sibling + 2 * n, 8)
        landed(ab.at[slot], ab_recv.at[slot])
    landed(nwin.at[pl.ds(0, 7)], nwin_recv)
    landed(gwin.at[pl.ds(0, 7)], gwin_recv)
    for copy in kept:
        copy.wait()
    tokens = (((0,), (0,)), ((), ()))
    both = ab[...].reshape(1024, 768)
    expanded = lax.dot_general(
        nwin[...].reshape(1024, 256), both[:, 384:], tokens, preferred_element_type=jnp.float32
    )
    odd = lax.rem(b, 2)
    reduced = lax.dot_general(
        both[:, :384], gwin[...].reshape(1024, 256), tokens, preferred_element_type=jnp.float32
    )

    @pl.when(odd == 0)
    def _():
        expand_ref[...] = expanded[:192]
        reduce_ref[...] = reduced[:, :192]

    @pl.when(odd == 1)
    def _():
        expand_ref[...] = expanded[64:]
        reduce_ref[...] = reduced[:, 64:]

    @pl.when(not_last)
    def _():
        row_copy(0, following).wait_send()
        row_copy(2, following).wait_send()

    @pl.when(not_first)
    def _():
        row_copy(1, preceding).wait_send()

    @pl.loop(1, 8)
    def _(j):
        wide_copy(pw, pw_send, pw_recv, j).wait_send()
        wide_copy(gw, gw_send, gw_recv, j).wait_send()
        sum_copy(j).wait_send()
        window_copy(nbuf, nwin, nwin_send, nwin_recv, j).wait_send()
        window_copy(gw, gwin, gwin_send, gwin_recv, j).wait_send()

    @pl.loop(1, 4)
    def _(j):
        same_core(j).wait_send()

    share(b, 0).wait_send()
    for j in range(1, 4):
        share(lax.rem(b + 2 * j, 8), j).wait_send()


def finish_step(token_ids, embedding, attended, head_mixer, expand_weight, reduce_weight, cotangent):
    vmem = pl.BlockSpec(memory_space=pltpu.VMEM)
    dma = pltpu.SemaphoreType.DMA
    f32, bf16 = jnp.float32, jnp.bfloat16
    return pl.pallas_call(
        middle_kernel,
        name="middle",
        out_shape=(
            jax.ShapeDtypeStruct((128, 1536), bf16),
            jax.ShapeDtypeStruct((192, 384), f32),
            jax.ShapeDtypeStruct((384, 192), f32),
        ),
        in_specs=[vmem] * 7,
        out_specs=(vmem,) * 3,
        scratch_shapes=[
            pltpu.VMEM((136, 1536), f32),
            pltpu.VMEM((24, 1536), f32),
            pltpu.VMEM((24, 1536), f32),
            pltpu.VMEM((3, 1, 1536), f32),
            pltpu.VMEM((3, 1, 1536), f32),
            pltpu.VMEM((128, 1536), bf16),
            pltpu.VMEM((128, 1536), bf16),
            pltpu.VMEM((128, 1536), bf16),
            pltpu.VMEM((128, 1536), bf16),
            pltpu.VMEM((7, 16, 1536), bf16),
            pltpu.VMEM((8, 128, 768), bf16),
            pltpu.VMEM((8, 128, 256), bf16),
            pltpu.VMEM((8, 128, 256), bf16),
            dma((3,)),
            dma((3,)),
            dma((7,)),
            dma((7,)),
            dma((7,)),
            dma((3,)),
            dma((4,)),
            dma((8,)),
            dma((8,)),
            dma,
            dma,
            dma,
            dma((8,)),
            dma,
            dma,
        ],
        compiler_params=pltpu.CompilerParams(collective_id=1, has_side_effects=True),
    )(
        token_ids.reshape(1, -1),
        embedding,
        attended,
        head_mixer,
        expand_weight,
        reduce_weight,
        cotangent,
    )


def local(
    token_ids,
    embedding,
    queries,
    key_rows,
    value_rows,
    head_mixer,
    expand_weight,
    reduce_weight,
    cotangent,
):
    attended = attention(queries, key_rows, value_rows)
    return finish_step(
        token_ids, embedding, attended, head_mixer, expand_weight, reduce_weight, cotangent
    )


def solution(mesh):
    return jax.shard_map(
        local,
        mesh=mesh,
        in_specs=(
            P(("dp", "blk", "wide")),
            P(),
            P(("dp", "blk", "wide"), None),
            P(("dp", "blk", "wide"), None),
            P(("dp", "blk", "wide"), None),
            P(),
            P(None, "wide"),
            P("wide", None),
            P(("dp", "blk", "wide"), None),
        ),
        out_specs=(
            P(("dp", "blk", "wide"), None),
            P(("dp", "blk"), "wide"),
            P(("dp", "wide"), "blk"),
        ),
        check_vma=False,
    )
```

```python
import jax
import jax.numpy as jnp
from jax import lax
from jax.experimental import pallas as pl
from jax.experimental.pallas import tpu as pltpu
from jax.sharding import PartitionSpec as P

FINE_HEADS = 6
HEAD = 128
VOCAB = 6


MESH = pl.DeviceIdType.MESH
ROUNDS = 8
RELAY, ACROSS, LAST = 2, 3, 4
LEAD = 3
SCALE = HEAD ** (-0.5) * 1.4426950408889634
MASKED = -2e38
EMPTY = -1e30


def offset_of(r):
    return (r + 1) // 2 * (2 * (r % 2) - 1)


def landed(ref, sem):
    pltpu.make_async_copy(ref, ref, sem).wait()


def gelu_parts(x):
    root = 0.7978845608028654
    inner = jnp.tanh(root * (x + 0.044715 * x * x * x))
    slope = 0.5 * (1.0 + inner) + 0.5 * x * (1.0 - inner * inner) * root * (
        1.0 + 3 * 0.044715 * x * x
    )
    return 0.5 * x * (1.0 + inner), slope


def step_kernel(
    tok_ref,
    emb_ref,
    q_ref,
    k_ref,
    v_ref,
    cot_ref,
    mixer_hbm,
    w1_hbm,
    w2_hbm,
    restored_ref,
    grads_ref,
    qbuf,
    kvbuf,
    acc,
    maxima,
    obuf,
    pobuf,
    abuf,
    pst,
    mixer_ref,
    w1_ref,
    w2_ref,
    lbuf,
    obuf16,
    mbuf,
    row_out,
    row_in,
    tok_in,
    cw,
    pw,
    gw,
    nbuf,
    pbuf,
    rsb,
    ab,
    nwin,
    gwin,
    sbuf,
    ready,
    w_sem,
    q_send,
    kv_send,
    own_send,
    relay_send,
    opp_send,
    o_send,
    po_send,
    px_send,
    q_recv,
    kv_recv,
    o_recv,
    po_recv,
    px_recv,
    row_send,
    row_recv,
    tok_send,
    tok_recv,
    cw_send,
    cw_recv,
    gw_send,
    rs_send,
    ab_send,
    sib_send,
    nwin_send,
    gwin_send,
    gw_recv,
    rs_recv,
    ab_recv,
    nwin_recv,
    gwin_recv,
):
    b = lax.axis_index("blk")
    z = lax.axis_index("wide")
    place = b * 8 + z
    sibling = b + 1 - 2 * lax.rem(b, 2)
    up = lax.rem(b + 2, 8)
    down = lax.rem(b + 6, 8)
    across = lax.rem(b + 4, 8)
    home = lax.rem(b + 3 * z, 8)
    holds_head = z < FINE_HEADS
    first, last = place == 0, place == 63
    not_first, not_last = place > 0, place < 63
    following = {"blk": lax.rem(b + (z + 1) // 8, 8), "wide": lax.rem(z + 1, 8)}
    preceding = {"blk": lax.rem(b + 8 - (8 - z) // 8, 8), "wide": lax.rem(z + 7, 8)}

    def holder(wide, h):
        return lax.rem(wide + 5 * h, 8)

    barrier = pltpu.get_barrier_semaphore()

    def greet(sem, where):
        pl.semaphore_signal(sem, inc=1, device_id=where, device_id_type=MESH)

    @pl.loop(1, 8)
    def _(j):
        greet(barrier, {"blk": b, "wide": lax.rem(z + j, 8)})
        greet(barrier, {"blk": lax.rem(b + j, 8), "wide": z})

    weights_in = [
        pltpu.make_async_copy(src, dst, w_sem.at[n])
        for n, (src, dst) in enumerate(
            ((mixer_hbm, mixer_ref), (w1_hbm, w1_ref), (w2_hbm, w2_ref))
        )
    ]
    for copy in weights_in:
        copy.start()

    def remote(src, dst, send, recv, where):
        return pltpu.make_async_remote_copy(
            src_ref=src,
            dst_ref=dst,
            send_sem=send,
            recv_sem=recv,
            device_id=where,
            device_id_type=MESH,
        )

    eight = lax.broadcasted_iota(jnp.int32, (8, 1536), 0)

    def at_row(n, row):
        return jnp.where(eight == n, jnp.broadcast_to(row, (8, 1536)), 0.0)

    def row_copy(n, where):
        return remote(row_out.at[n], row_in.at[n], row_send.at[n], row_recv.at[n], where)

    def tok_copy():
        return remote(tok_ref, tok_in, tok_send, tok_recv, following)

    short = lax.broadcasted_iota(jnp.int32, (16, 128), 0)
    inside = lax.broadcasted_iota(jnp.int32, (16, 128), 1) - 8 * short
    own = jnp.logical_and(inside >= 0, inside < 8)
    inside = inside.astype(jnp.float32)
    after = jnp.where(own, (inside + 1.0) / 8, 0.0).astype(jnp.bfloat16)
    before = jnp.where(own, (7.0 - inside) / 8, 0.0).astype(jnp.bfloat16)
    cot = cot_ref[...]
    later_part = jnp.dot(before, cot, preferred_element_type=jnp.float32)
    lbuf[:16] = later_part
    row_out[0] = later_part[:1]
    obuf16[...] = jnp.dot(after, cot, preferred_element_type=jnp.float32)
    acc[...] = jnp.zeros_like(acc)
    maxima[...] = jnp.full_like(maxima, EMPTY)

    @pl.when(last)
    def _():
        row_in[0] = jnp.zeros((1, 1536), jnp.float32)

    @pl.when(first)
    def _():
        row_in[1] = jnp.zeros((1, 1536), jnp.float32)
        tok_in[...] = jnp.full((1, 128), -1, jnp.int32)

    @pl.when(b == 0)
    def _():
        pst[256:] = jnp.zeros((16, 768), jnp.bfloat16)

    pl.semaphore_wait(barrier, 14)
    mine = pl.ds(pl.multiple_of(z * 16, 16), 16)

    def wide_copy(buf, send, recv, j):
        where = {"blk": b, "wide": lax.rem(z + j, 8)}
        return remote(buf.at[mine], buf.at[mine], send.at[j - 1], recv, where)

    def count_copy(j):
        where = {"blk": b, "wide": lax.rem(z + j, 8)}
        return remote(cw.at[z], cw.at[z], cw_send.at[j - 1], cw_recv, where)

    def send_grads():
        @pl.when(not_last)
        def _():
            landed(row_in.at[0], row_recv.at[0])

        lbuf[16:] = at_row(0, row_in[0])
        gw[mine, :] = (obuf16[...] + lbuf[1:17]).astype(jnp.bfloat16)

        @pl.loop(1, 8)
        def _(j):
            wide_copy(gw, gw_send, gw_recv, j).start()

        @pl.when(not_first)
        def _():
            landed(tok_in, tok_recv)

        lane = lax.broadcasted_iota(jnp.int32, (128, 128), 1)
        kind = lax.broadcasted_iota(jnp.int32, (128, 128), 0)
        shifted = jnp.where(
            lane == 0,
            pltpu.roll(jnp.broadcast_to(tok_in[...], (128, 128)), 1, 1),
            pltpu.roll(jnp.broadcast_to(tok_ref[...], (128, 128)), 1, 1),
        )
        short = lax.broadcasted_iota(jnp.int32, (16, 128), 0)
        inside = lax.broadcasted_iota(jnp.int32, (16, 128), 1) - 8 * short
        eighth = jnp.where(jnp.logical_and(inside >= 0, inside < 8), 0.125, 0.0)
        cw[z] = lax.dot_general(
            eighth.astype(jnp.bfloat16),
            jnp.where(kind == shifted, 1.0, 0.0).astype(jnp.bfloat16),
            (((1,), (1,)), ((), ())),
            preferred_element_type=jnp.float32,
        ).astype(jnp.bfloat16)

        @pl.loop(1, 8)
        def _(j):
            count_copy(j).start()

    def head_columns(h):
        return pl.ds(pl.multiple_of(h * HEAD, HEAD), HEAD)

    def kv_copies(r, h):
        copies = []
        for n, ref in enumerate((k_ref, v_ref)):
            copies.append(
                pltpu.make_async_remote_copy(
                    src_ref=ref.at[:, head_columns(h)],
                    dst_ref=kvbuf.at[r, n, b],
                    send_sem=kv_send.at[r, n],
                    recv_sem=kv_recv.at[r, b],
                    device_id={"blk": b, "wide": h},
                    device_id_type=MESH,
                )
            )
        return copies

    def q_copy(h):
        return pltpu.make_async_remote_copy(
            src_ref=q_ref.at[:, head_columns(h)],
            dst_ref=qbuf.at[b],
            send_sem=q_send.at[h],
            recv_sem=q_recv.at[b],
            device_id={"blk": holder(z, h), "wide": h},
            device_id_type=MESH,
        )

    def q_local():
        return pltpu.make_async_copy(q_ref.at[:, head_columns(z)], qbuf.at[b], q_recv.at[b])

    def is_self(h):
        return jnp.logical_and(z == home, h == z)

    @pl.when(z < FINE_HEADS)
    def _():
        for n, ref in enumerate((k_ref, v_ref)):
            pltpu.make_async_copy(
                ref.at[:, head_columns(z)], kvbuf.at[0, n, b], kv_recv.at[0, b]
            ).start()

    def send_round(r):
        h = lax.rem(z - offset_of(r) + 8, 8)

        @pl.when(h < FINE_HEADS)
        def _():
            for copy in kv_copies(r, h):
                copy.start()

    def wait_round(r):
        h = lax.rem(z - offset_of(r) + 8, 8)

        @pl.when(h < FINE_HEADS)
        def _():
            for copy in kv_copies(r, h):
                copy.wait_send()

    for r in range(1, LEAD + 1):
        send_round(r)

    def send_queries():
        @pl.loop(0, FINE_HEADS)
        def _(h):
            @pl.when(is_self(h))
            def _():
                q_local().start()

            @pl.when(jnp.logical_not(is_self(h)))
            def _():
                q_copy(h).start()

    @pl.loop(1, 8)
    def _(j):
        greet(ready, {"blk": lax.rem(b + j, 8), "wide": z})

    pl.semaphore_wait(ready, 7)
    send_queries()

    @pl.when(not_last)
    def _():
        tok_copy().start()

    @pl.when(not_first)
    def _():
        row_copy(0, preceding).start()

    @pl.when(jnp.logical_not(holds_head))
    def _():
        @pl.loop(1, ROUNDS)
        def _(r):
            wait_round(r)

            @pl.when(r < ROUNDS - LEAD)
            def _():
                send_round(r + LEAD)

        send_grads()

    def piece(r, blk):
        return kvbuf.at[r, :, blk]

    def pass_on(src, sem, recv, blk):
        return pltpu.make_async_remote_copy(
            src_ref=src,
            dst_ref=src,
            send_sem=sem,
            recv_sem=recv,
            device_id={"blk": blk, "wide": z},
            device_id_type=MESH,
        )

    def own_copies(r):
        recv = kv_recv.at[r, b]
        return [
            pass_on(piece(r, b), own_send.at[r, n], recv, blk)
            for n, blk in enumerate((up, down, sibling))
        ]

    def relay_copies(r):
        return [
            [
                pass_on(kvbuf.at[r, 0, down], relay_send.at[r, 0], kv_recv.at[r, down], up),
                pass_on(piece(r, down), relay_send.at[r, 1], kv_recv.at[r, down], sibling),
            ],
            [
                pass_on(kvbuf.at[r, 1, up], relay_send.at[r, 2], kv_recv.at[r, up], down),
                pass_on(piece(r, up), relay_send.at[r, 3], kv_recv.at[r, up], sibling),
            ],
        ]

    def opp_copy(r):
        return pass_on(piece(r, across), opp_send.at[r], kv_recv.at[r, across], sibling)

    def compute(r):
        source = lax.rem(z + offset_of(r) + 8, 8)
        rows = lax.broadcasted_iota(jnp.int32, (HEAD, HEAD), 0)
        cols = lax.broadcasted_iota(jnp.int32, (HEAD, HEAD), 1)
        allowed = cols + (source - home) * HEAD <= rows
        for n in range(8):
            keys = kvbuf[r, 0, : n + 1].reshape((n + 1) * HEAD, HEAD)
            values = kvbuf[r, 1, : n + 1].reshape((n + 1) * HEAD, HEAD)
            scores = lax.dot_general(
                qbuf[n], keys, (((1,), (1,)), ((), ())), preferred_element_type=jnp.float32
            )
            last = jnp.where(allowed, scores[:, n * HEAD :], MASKED)
            if n:
                scores = jnp.concatenate([scores[:, : n * HEAD], last], 1)
            else:
                scores = last
            before = maxima[n]
            highest = jnp.maximum(before, scores.max(-1, keepdims=True) * SCALE)
            weights = jnp.exp2(scores * SCALE - jnp.concatenate([highest] * (n + 1), 1))
            factor = jnp.exp2(before - highest)
            extended = jnp.concatenate([values, jnp.ones_like(values)], 1)
            summed = jnp.dot(
                weights.astype(jnp.bfloat16), extended, preferred_element_type=jnp.float32
            )
            acc[n] = acc[n] * jnp.concatenate([factor, factor], 1) + summed
            maxima[n] = highest

    def o_copy(n):
        return pltpu.make_async_remote_copy(
            src_ref=obuf.at[n],
            dst_ref=abuf.at[:, head_columns(z)],
            send_sem=o_send.at[n],
            recv_sem=o_recv,
            device_id={"blk": n, "wide": home},
            device_id_type=MESH,
        )

    def o_local(n):
        return pltpu.make_async_copy(obuf.at[n], abuf.at[:, head_columns(z)], o_recv)

    def pool_target():
        return pst.at[pl.ds(pl.multiple_of(home * 32, 32), 32), head_columns(z)]

    def pool_copy(n, w):
        return remote(
            pobuf.at[n], pool_target(), po_send.at[n, w], po_recv, {"blk": n, "wide": w}
        )

    def pool_local(n):
        return pltpu.make_async_copy(pobuf.at[n], pool_target(), po_recv)

    def edge_copy(n, w):
        return remote(
            pobuf.at[n, pl.ds(16, 16)],
            pst.at[pl.ds(256, 16), head_columns(z)],
            px_send.at[n, w],
            px_recv,
            {"blk": n + 1, "wide": w},
        )

    def edge_local(n):
        return pltpu.make_async_copy(
            pobuf.at[n, pl.ds(16, 16)], pst.at[pl.ds(256, 16), head_columns(z)], px_recv
        )

    def is_next(n, w):
        return jnp.logical_and(n + 1 == b, w == z)

    @pl.when(z < FINE_HEADS)
    def _():
        @pl.loop(0, ROUNDS + LAST)
        def _(i):
            def stage(late):
                return jnp.logical_and(i >= late, i < ROUNDS + late)

            @pl.when(i < ROUNDS)
            def _():
                landed(piece(i, b), kv_recv.at[i, b])

                @pl.when(jnp.logical_and(i > 0, i < ROUNDS - LEAD))
                def _():
                    send_round(i + LEAD)

                for copy in own_copies(i):
                    copy.start()

            @pl.when(stage(RELAY))
            def _():
                r = i - RELAY
                first, second = relay_copies(r)
                landed(piece(r, down), kv_recv.at[r, down])
                for copy in first:
                    copy.start()
                landed(piece(r, up), kv_recv.at[r, up])
                for copy in second:
                    copy.start()

            @pl.when(stage(ACROSS))
            def _():
                r = i - ACROSS
                landed(piece(r, across), kv_recv.at[r, across])
                opp_copy(r).start()

            @pl.when(i == LAST)
            def _():
                send_grads()
                for n in range(8):
                    landed(qbuf.at[n], q_recv.at[n])

            @pl.when(i >= LAST)
            def _():
                r = i - LAST
                for n in range(4):
                    other = lax.rem(sibling + 2 * n, 8)
                    landed(piece(r, other), kv_recv.at[r, other])
                compute(r)

        short = lax.broadcasted_iota(jnp.int32, (32, HEAD), 0)
        inside = lax.broadcasted_iota(jnp.int32, (32, HEAD), 1) - 8 * short
        taken = jnp.where(
            short < 16,
            jnp.logical_and(inside >= -1, inside < 7).astype(jnp.int32),
            jnp.logical_and(short == 16, inside == -1).astype(jnp.int32),
        )
        pool = jnp.where(taken == 1, 0.125, 0.0).astype(jnp.bfloat16)
        for n in range(8):
            total = acc[n]
            out = (total[:, :HEAD] / total[:, HEAD:]).astype(jnp.bfloat16)
            obuf[n] = out
            pobuf[n] = jnp.dot(pool, out, preferred_element_type=jnp.float32).astype(jnp.bfloat16)

            @pl.loop(0, 8)
            def _(w):
                at_self = jnp.logical_and(n == b, w == z)

                @pl.when(at_self)
                def _():
                    pool_local(n).start()

                @pl.when(jnp.logical_not(at_self))
                def _():
                    pool_copy(n, w).start()

                if n < 7:
                    crosses = home == 7

                    @pl.when(jnp.logical_and(crosses, is_next(n, w)))
                    def _():
                        edge_local(n).start()

                    @pl.when(jnp.logical_and(crosses, jnp.logical_not(is_next(n, w))))
                    def _():
                        edge_copy(n, w).start()

        for n in range(8):
            here = jnp.logical_and(n == b, z == home)

            @pl.when(here)
            def _():
                o_local(n).start()

            @pl.when(jnp.logical_not(here))
            def _():
                o_copy(n).start()

    landed(gw.at[pl.ds(0, 112)], gw_recv)
    def same_core(j):
        return remote(
            ab.at[b],
            ab.at[b],
            ab_send.at[j - 1],
            ab_recv.at[b],
            {"blk": lax.rem(b + 2 * j, 8), "wide": z},
        )

    def share(slot, n):
        return remote(
            ab.at[slot], ab.at[slot], sib_send.at[n], ab_recv.at[slot], {"blk": sibling, "wide": z}
        )

    def window(ref, to):
        return ref.at[:, pl.ds(pl.multiple_of(to * 192 // 128 * 128, 128), 256)]

    def window_copy(src, dst, send, recv, j):
        to = lax.rem(b + j, 8)
        return remote(
            window(src, to), dst.at[b], send.at[j - 1], recv, {"blk": to, "wide": z}
        )

    kept = [
        pltpu.make_async_copy(window(nbuf, b), nwin.at[b], nwin_send.at[7]),
        pltpu.make_async_copy(window(gw, b), gwin.at[b], gwin_send.at[7]),
    ]
    kept[1].start()

    @pl.loop(1, 8)
    def _(j):
        window_copy(gw, gwin, gwin_send, gwin_recv, j).start()

    for copy in weights_in:
        copy.wait()
    act_grad = lax.dot_general(
        gw[...], w2_ref[...], (((1,), (1,)), ((), ())), preferred_element_type=jnp.float32
    )

    landed(cw.at[pl.ds(0, 7)], cw_recv)
    counts = cw[...].reshape(128, 128)[:, :VOCAB].astype(jnp.float32)
    embedded = jnp.dot(
        counts,
        emb_ref[...],
        precision=lax.Precision.HIGHEST,
        preferred_element_type=jnp.float32,
    )
    row = lax.broadcasted_iota(jnp.int32, (128, 272), 0)
    col = lax.broadcasted_iota(jnp.int32, (128, 272), 1)
    group = lax.shift_right_logical(row, 4)
    within = jnp.bitwise_and(row, 15)
    edge = jnp.where(group == 0, 256, 32 * group - 16)
    picked = jnp.logical_or(
        col == 32 * group + within, jnp.logical_and(within == 0, col == edge)
    )
    picked = jnp.where(picked, 1.0, 0.0).astype(jnp.bfloat16)

    @pl.when(b > 0)
    def _():
        landed(pst.at[pl.ds(256, 16)], px_recv)

    landed(pst.at[pl.ds(0, 256)], po_recv)
    gathered = jnp.dot(picked, pst[...], preferred_element_type=jnp.float32).astype(jnp.bfloat16)
    pooled = embedded + jnp.dot(gathered, mixer_ref[...], preferred_element_type=jnp.float32)
    pooled = pooled.astype(jnp.bfloat16)
    pw[...] = pooled
    pooled_wide = pooled.astype(jnp.float32)
    scale = lax.rsqrt(jnp.mean(pooled_wide * pooled_wide, -1, keepdims=True) + 1e-06)
    normed = (pooled_wide * scale).astype(jnp.bfloat16)
    nbuf[...] = normed
    expanded = jnp.dot(normed, w1_ref[...], preferred_element_type=jnp.float32)
    activated, slope = gelu_parts(expanded)
    activated = activated.astype(jnp.bfloat16)
    pbuf[...] = jnp.dot(
        activated, w2_ref[...], preferred_element_type=jnp.float32
    ).astype(jnp.bfloat16)

    def sum_copy(j):
        to = lax.rem(z + j, 8)
        return remote(
            pbuf.at[pl.ds(pl.multiple_of(to * 16, 16), 16)],
            rsb.at[j - 1],
            rs_send.at[j - 1],
            rs_recv,
            {"blk": b, "wide": to},
        )

    @pl.loop(1, 8)
    def _(j):
        sum_copy(j).start()

    ab[b, :, :384] = activated
    ab[b, :, 384:] = (act_grad * slope).astype(jnp.bfloat16)

    @pl.loop(1, 4)
    def _(j):
        same_core(j).start()

    share(b, 0).start()
    kept[0].start()

    @pl.loop(1, 8)
    def _(j):
        window_copy(nbuf, nwin, nwin_send, nwin_recv, j).start()

    kind = lax.broadcasted_iota(jnp.int32, (VOCAB, 128), 0)
    onehot = (kind == tok_ref[...]).astype(jnp.float32)
    stream = lax.dot_general(
        onehot,
        emb_ref[...],
        (((0,), (0,)), ((), ())),
        precision=lax.Precision.HIGHEST,
        preferred_element_type=jnp.float32,
    )
    landed(abuf, o_recv)
    sbuf[...] = stream + jnp.dot(
        abuf[...], mixer_ref[...], preferred_element_type=jnp.float32
    )

    landed(rsb, rs_recv)
    middle = pw[mine, :].astype(jnp.float32) + pbuf[mine, :].astype(jnp.float32)
    for n in range(7):
        middle = middle + rsb[n].astype(jnp.float32)
    mbuf[8:] = middle
    row_out[1] = middle[15:]

    @pl.when(not_last)
    def _():
        row_copy(1, following).start()

    for j in range(1, 4):
        slot = lax.rem(b + 2 * j, 8)
        landed(ab.at[slot], ab_recv.at[slot])
        share(slot, j).start()

    @pl.when(not_first)
    def _():
        landed(row_in.at[1], row_recv.at[1])

    mbuf[:8] = at_row(7, row_in[1])
    steps = lax.broadcasted_iota(jnp.int32, (8, 1536), 0).astype(jnp.float32)
    ahead, behind = (steps + 1.0) / 8, (7.0 - steps) / 8
    for j in range(0, 16, 2):
        rows = [
            sbuf[8 * n : 8 * (n + 1)]
            + mbuf[8 + n : 9 + n] * ahead
            + mbuf[7 + n : 8 + n] * behind
            for n in (j, j + 1)
        ]
        restored_ref[8 * j : 8 * (j + 2)] = jnp.concatenate(rows, 0).astype(jnp.bfloat16)

    for n in range(4):
        slot = lax.rem(sibling + 2 * n, 8)
        landed(ab.at[slot], ab_recv.at[slot])
    landed(nwin.at[pl.ds(0, 7)], nwin_recv)
    landed(gwin.at[pl.ds(0, 7)], gwin_recv)
    for copy in kept:
        copy.wait()
    tokens = (((0,), (0,)), ((), ()))
    both = ab[...].reshape(1024, 768)
    expanded = lax.dot_general(
        nwin[...].reshape(1024, 256), both[:, 384:], tokens, preferred_element_type=jnp.float32
    )
    odd = lax.rem(b, 2)
    reduced = lax.dot_general(
        gwin[...].reshape(1024, 256), both[:, :384], tokens, preferred_element_type=jnp.float32
    )

    @pl.when(odd == 0)
    def _():
        grads_ref[0] = expanded[:192]
        grads_ref[1] = reduced[:192]

    @pl.when(odd == 1)
    def _():
        grads_ref[0] = expanded[64:]
        grads_ref[1] = reduced[64:]

    @pl.when(holds_head)
    def _():
        @pl.loop(0, ROUNDS)
        def _(r):
            for copy in own_copies(r):
                copy.wait_send()
            for pair in relay_copies(r):
                for copy in pair:
                    copy.wait_send()
            opp_copy(r).wait_send()

        @pl.loop(1, ROUNDS)
        def _(r):
            wait_round(r)

        @pl.loop(0, 8)
        def _(n):
            @pl.when(jnp.logical_not(jnp.logical_and(n == b, z == home)))
            def _():
                o_copy(n).wait_send()

            @pl.loop(0, 8)
            def _(w):
                @pl.when(jnp.logical_not(jnp.logical_and(n == b, w == z)))
                def _():
                    pool_copy(n, w).wait_send()

                @pl.when(
                    jnp.logical_and(
                        jnp.logical_and(home == 7, n < 7), jnp.logical_not(is_next(n, w))
                    )
                )
                def _():
                    edge_copy(n, w).wait_send()

    @pl.loop(0, FINE_HEADS)
    def _(h):
        @pl.when(jnp.logical_not(is_self(h)))
        def _():
            q_copy(h).wait_send()

    @pl.when(not_last)
    def _():
        row_copy(1, following).wait_send()
        tok_copy().wait_send()

    @pl.when(not_first)
    def _():
        row_copy(0, preceding).wait_send()

    @pl.loop(1, 8)
    def _(j):
        count_copy(j).wait_send()
        wide_copy(gw, gw_send, gw_recv, j).wait_send()
        sum_copy(j).wait_send()
        window_copy(nbuf, nwin, nwin_send, nwin_recv, j).wait_send()
        window_copy(gw, gwin, gwin_send, gwin_recv, j).wait_send()

    @pl.loop(1, 4)
    def _(j):
        same_core(j).wait_send()

    share(b, 0).wait_send()
    for j in range(1, 4):
        share(lax.rem(b + 2 * j, 8), j).wait_send()


def whole_step(*arrays):
    rows = 128
    vmem = pl.BlockSpec(memory_space=pltpu.VMEM)
    hbm = pl.BlockSpec(memory_space=pl.ANY)
    dma = pltpu.SemaphoreType.DMA
    f32, bf16 = jnp.float32, jnp.bfloat16
    return pl.pallas_call(
        step_kernel,
        name="step",
        out_shape=(
            jax.ShapeDtypeStruct((rows, 1536), bf16),
            jax.ShapeDtypeStruct((2, 192, 384), f32),
        ),
        in_specs=[vmem] * 6 + [hbm] * 3,
        out_specs=(vmem, vmem),
        scratch_shapes=[
            pltpu.VMEM((8, rows, HEAD), bf16),
            pltpu.VMEM((ROUNDS, 2, 8, rows, HEAD), bf16),
            pltpu.VMEM((8, rows, 2 * HEAD), f32),
            pltpu.VMEM((8, rows, HEAD), f32),
            pltpu.VMEM((8, rows, HEAD), bf16),
            pltpu.VMEM((8, 32, HEAD), bf16),
            pltpu.VMEM((rows, 768), bf16),
            pltpu.VMEM((272, 768), bf16),
            pltpu.VMEM((768, 1536), bf16),
            pltpu.VMEM((1536, 384), bf16),
            pltpu.VMEM((384, 1536), bf16),
            pltpu.VMEM((24, 1536), f32),
            pltpu.VMEM((16, 1536), f32),
            pltpu.VMEM((24, 1536), f32),
            pltpu.VMEM((2, 1, 1536), f32),
            pltpu.VMEM((2, 1, 1536), f32),
            pltpu.VMEM((1, 128), jnp.int32),
            pltpu.VMEM((8, 16, 128), bf16),
            pltpu.VMEM((128, 1536), bf16),
            pltpu.VMEM((128, 1536), bf16),
            pltpu.VMEM((128, 1536), bf16),
            pltpu.VMEM((128, 1536), bf16),
            pltpu.VMEM((7, 16, 1536), bf16),
            pltpu.VMEM((8, 128, 768), bf16),
            pltpu.VMEM((8, 128, 256), bf16),
            pltpu.VMEM((8, 128, 256), bf16),
            pltpu.VMEM((128, 1536), f32),
            pltpu.SemaphoreType.REGULAR,
            dma((3,)),
            dma((FINE_HEADS,)),
            dma((ROUNDS, 2)),
            dma((ROUNDS, 3)),
            dma((ROUNDS, 4)),
            dma((ROUNDS,)),
            dma((8,)),
            dma((8, 8)),
            dma((8, 8)),
            dma((8,)),
            dma((ROUNDS, 8)),
            dma,
            dma,
            dma,
            dma((2,)),
            dma((2,)),
            dma,
            dma,
            dma((7,)),
            dma,
            dma((7,)),
            dma((7,)),
            dma((3,)),
            dma((4,)),
            dma((8,)),
            dma((8,)),
            dma,
            dma,
            dma((8,)),
            dma,
            dma,
        ],
        compiler_params=pltpu.CompilerParams(collective_id=0, has_side_effects=True),
    )(*arrays)


def local(
    token_ids,
    embedding,
    queries,
    key_rows,
    value_rows,
    head_mixer,
    expand_weight,
    reduce_weight,
    cotangent,
):
    restored, grads = whole_step(
        token_ids.reshape(1, -1),
        embedding,
        queries,
        key_rows,
        value_rows,
        cotangent,
        head_mixer,
        expand_weight,
        reduce_weight,
    )
    return restored, grads[0], grads[1].T


def solution(mesh):
    return jax.shard_map(
        local,
        mesh=mesh,
        in_specs=(
            P(("dp", "blk", "wide")),
            P(),
            P(("dp", "blk", "wide"), None),
            P(("dp", "blk", "wide"), None),
            P(("dp", "blk", "wide"), None),
            P(),
            P(None, "wide"),
            P("wide", None),
            P(("dp", "blk", "wide"), None),
        ),
        out_specs=(
            P(("dp", "blk", "wide"), None),
            P(("dp", "blk"), "wide"),
            P(("dp", "wide"), "blk"),
        ),
        check_vma=False,
    )
```

```python
import jax
import jax.numpy as jnp
from jax import lax
from jax.experimental import pallas as pl
from jax.experimental.pallas import tpu as pltpu
from jax.sharding import PartitionSpec as P

FINE_HEADS = 6
HEAD = 128
VOCAB = 6


MESH = pl.DeviceIdType.MESH
ROUNDS = 8
RELAY, ACROSS, LAST = 2, 4, 5
LEAD = 3
GRADS = 5
SCALE = HEAD ** (-0.5) * 1.4426950408889634
MASKED = -2e38
EMPTY = -1e30


def offset_of(r):
    return (r + 1) // 2 * (2 * (r % 2) - 1)


def landed(ref, sem):
    pltpu.make_async_copy(ref, ref, sem).wait()


def gelu_parts(x):
    root = 0.7978845608028654
    inner = jnp.tanh(root * (x + 0.044715 * x * x * x))
    slope = 0.5 * (1.0 + inner) + 0.5 * x * (1.0 - inner * inner) * root * (
        1.0 + 3 * 0.044715 * x * x
    )
    return 0.5 * x * (1.0 + inner), slope


def step_kernel(
    tok_ref,
    emb_ref,
    q_hbm,
    k_hbm,
    v_hbm,
    cot_hbm,
    mixer_hbm,
    w1_hbm,
    w2_hbm,
    restored_ref,
    expand_ref,
    reduce_ref,
    q_ref,
    k_ref,
    v_ref,
    cot_ref,
    qbuf,
    kvbuf,
    acc,
    maxima,
    obuf,
    pobuf,
    abuf,
    pst,
    ph,
    poh,
    mixer_ref,
    w1_ref,
    w2_ref,
    lbuf,
    obuf16,
    mbuf,
    row_out,
    row_in,
    tok_in,
    cw,
    pw,
    gw,
    nbuf,
    pbuf,
    rsb,
    ab,
    nwin,
    gwin,
    sbuf,
    ready,
    w_sem,
    q_send,
    kv_send,
    own_send,
    relay_send,
    opp_send,
    o_send,
    po_send,
    px_send,
    pg_send,
    q_recv,
    kv_recv,
    o_recv,
    po_recv,
    ph_recv,
    px_recv,
    row_send,
    row_recv,
    tok_send,
    tok_recv,
    cw_send,
    cw_recv,
    gw_send,
    rs_send,
    ab_send,
    sib_send,
    nwin_send,
    gwin_send,
    gw_recv,
    rs_recv,
    ab_recv,
    nwin_recv,
    gwin_recv,
):
    b = lax.axis_index("blk")
    z = lax.axis_index("wide")
    place = b * 8 + z
    sibling = b + 1 - 2 * lax.rem(b, 2)
    up = lax.rem(b + 2, 8)
    down = lax.rem(b + 6, 8)
    across = lax.rem(b + 4, 8)
    home = lax.rem(b + 3 * z, 8)
    holds_head = z < FINE_HEADS
    first, last = place == 0, place == 63
    not_first, not_last = place > 0, place < 63
    following = {"blk": lax.rem(b + (z + 1) // 8, 8), "wide": lax.rem(z + 1, 8)}
    preceding = {"blk": lax.rem(b + 8 - (8 - z) // 8, 8), "wide": lax.rem(z + 7, 8)}

    def holder(wide, h):
        return lax.rem(wide + 5 * h, 8)

    barrier = pltpu.get_barrier_semaphore()

    def greet(sem, where):
        pl.semaphore_signal(sem, inc=1, device_id=where, device_id_type=MESH)

    @pl.loop(1, 8)
    def _(j):
        greet(barrier, {"blk": b, "wide": lax.rem(z + j, 8)})
        greet(barrier, {"blk": lax.rem(b + j, 8), "wide": z})

    weights_in = [
        pltpu.make_async_copy(src, dst, w_sem.at[n])
        for n, (src, dst) in enumerate(
            ((mixer_hbm, mixer_ref), (w1_hbm, w1_ref), (w2_hbm, w2_ref))
        )
    ]
    rows_in = [
        pltpu.make_async_copy(src, dst, w_sem.at[n + 3])
        for n, (src, dst) in enumerate(
            ((k_hbm, k_ref), (v_hbm, v_ref), (q_hbm, q_ref), (cot_hbm, cot_ref))
        )
    ]
    for copy in rows_in:
        copy.start()

    def remote(src, dst, send, recv, where):
        return pltpu.make_async_remote_copy(
            src_ref=src,
            dst_ref=dst,
            send_sem=send,
            recv_sem=recv,
            device_id=where,
            device_id_type=MESH,
        )

    eight = lax.broadcasted_iota(jnp.int32, (8, 1536), 0)

    def at_row(n, row):
        return jnp.where(eight == n, jnp.broadcast_to(row, (8, 1536)), 0.0)

    def row_copy(n, where):
        return remote(row_out.at[n], row_in.at[n], row_send.at[n], row_recv.at[n], where)

    def tok_copy():
        return remote(tok_ref, tok_in, tok_send, tok_recv, following)

    short = lax.broadcasted_iota(jnp.int32, (16, 128), 0)
    inside = lax.broadcasted_iota(jnp.int32, (16, 128), 1) - 8 * short
    own = jnp.logical_and(inside >= 0, inside < 8)
    inside = inside.astype(jnp.float32)
    after = jnp.where(own, (inside + 1.0) / 8, 0.0).astype(jnp.bfloat16)
    before = jnp.where(own, (7.0 - inside) / 8, 0.0).astype(jnp.bfloat16)
    rows_in[3].wait()
    cot = cot_ref[...]
    later_part = jnp.dot(before, cot, preferred_element_type=jnp.float32)
    lbuf[:16] = later_part
    row_out[0] = later_part[:1]
    obuf16[...] = jnp.dot(after, cot, preferred_element_type=jnp.float32)
    acc[...] = jnp.zeros_like(acc)
    maxima[...] = jnp.full_like(maxima, EMPTY)

    @pl.when(last)
    def _():
        row_in[0] = jnp.zeros((1, 1536), jnp.float32)

    @pl.when(first)
    def _():
        row_in[1] = jnp.zeros((1, 1536), jnp.float32)
        tok_in[...] = jnp.full((1, 128), -1, jnp.int32)

    @pl.when(b == 0)
    def _():
        ph[256:] = jnp.zeros((16, HEAD), jnp.bfloat16)

    for copy in rows_in[:3]:
        copy.wait()
    pl.semaphore_wait(barrier, 14)
    mine = pl.ds(pl.multiple_of(z * 16, 16), 16)

    def wide_copy(buf, send, recv, j):
        where = {"blk": b, "wide": lax.rem(z + j, 8)}
        return remote(buf.at[mine], buf.at[mine], send.at[j - 1], recv, where)

    def count_copy(j):
        where = {"blk": b, "wide": lax.rem(z + j, 8)}
        return remote(cw.at[z], cw.at[z], cw_send.at[j - 1], cw_recv, where)

    def send_grads():
        @pl.when(not_last)
        def _():
            landed(row_in.at[0], row_recv.at[0])

        lbuf[16:] = at_row(0, row_in[0])
        gw[mine, :] = (obuf16[...] + lbuf[1:17]).astype(jnp.bfloat16)

        @pl.loop(1, 8)
        def _(j):
            wide_copy(gw, gw_send, gw_recv, j).start()

        @pl.when(not_first)
        def _():
            landed(tok_in, tok_recv)

        lane = lax.broadcasted_iota(jnp.int32, (128, 128), 1)
        kind = lax.broadcasted_iota(jnp.int32, (128, 128), 0)
        shifted = jnp.where(
            lane == 0,
            pltpu.roll(jnp.broadcast_to(tok_in[...], (128, 128)), 1, 1),
            pltpu.roll(jnp.broadcast_to(tok_ref[...], (128, 128)), 1, 1),
        )
        short = lax.broadcasted_iota(jnp.int32, (16, 128), 0)
        inside = lax.broadcasted_iota(jnp.int32, (16, 128), 1) - 8 * short
        eighth = jnp.where(jnp.logical_and(inside >= 0, inside < 8), 0.125, 0.0)
        cw[z] = lax.dot_general(
            eighth.astype(jnp.bfloat16),
            jnp.where(kind == shifted, 1.0, 0.0).astype(jnp.bfloat16),
            (((1,), (1,)), ((), ())),
            preferred_element_type=jnp.float32,
        ).astype(jnp.bfloat16)

        @pl.loop(1, 8)
        def _(j):
            count_copy(j).start()

    def head_columns(h):
        return pl.ds(pl.multiple_of(h * HEAD, HEAD), HEAD)

    def kv_copies(r, h):
        copies = []
        for n, ref in enumerate((k_ref, v_ref)):
            copies.append(
                pltpu.make_async_remote_copy(
                    src_ref=ref.at[:, head_columns(h)],
                    dst_ref=kvbuf.at[r, n, b],
                    send_sem=kv_send.at[r, n],
                    recv_sem=kv_recv.at[r, b],
                    device_id={"blk": b, "wide": h},
                    device_id_type=MESH,
                )
            )
        return copies

    def q_copy(h):
        return pltpu.make_async_remote_copy(
            src_ref=q_ref.at[:, head_columns(h)],
            dst_ref=qbuf.at[b],
            send_sem=q_send.at[h],
            recv_sem=q_recv.at[b],
            device_id={"blk": holder(z, h), "wide": h},
            device_id_type=MESH,
        )

    def q_local():
        return pltpu.make_async_copy(q_ref.at[:, head_columns(z)], qbuf.at[b], q_recv.at[b])

    def is_self(h):
        return jnp.logical_and(z == home, h == z)

    @pl.when(z < FINE_HEADS)
    def _():
        for n, ref in enumerate((k_ref, v_ref)):
            pltpu.make_async_copy(
                ref.at[:, head_columns(z)], kvbuf.at[0, n, b], kv_recv.at[0, b]
            ).start()

    def send_round(r):
        h = lax.rem(z - offset_of(r) + 8, 8)

        @pl.when(h < FINE_HEADS)
        def _():
            for copy in kv_copies(r, h):
                copy.start()

    def wait_round(r):
        h = lax.rem(z - offset_of(r) + 8, 8)

        @pl.when(h < FINE_HEADS)
        def _():
            for copy in kv_copies(r, h):
                copy.wait_send()

    for r in range(1, LEAD + 1):
        send_round(r)

    def send_queries():
        @pl.loop(0, FINE_HEADS)
        def _(h):
            @pl.when(is_self(h))
            def _():
                q_local().start()

            @pl.when(jnp.logical_not(is_self(h)))
            def _():
                q_copy(h).start()

    @pl.loop(1, 8)
    def _(j):
        greet(ready, {"blk": lax.rem(b + j, 8), "wide": z})

    for copy in weights_in:
        copy.start()
    pl.semaphore_wait(ready, 7)
    send_queries()

    @pl.when(not_last)
    def _():
        tok_copy().start()

    @pl.when(not_first)
    def _():
        row_copy(0, preceding).start()

    @pl.when(jnp.logical_not(holds_head))
    def _():
        @pl.loop(1, ROUNDS)
        def _(r):
            wait_round(r)

            @pl.when(r < ROUNDS - LEAD)
            def _():
                send_round(r + LEAD)

        send_grads()

    def piece(r, blk):
        return kvbuf.at[r, :, blk]

    def pass_on(src, sem, recv, blk):
        return pltpu.make_async_remote_copy(
            src_ref=src,
            dst_ref=src,
            send_sem=sem,
            recv_sem=recv,
            device_id={"blk": blk, "wide": z},
            device_id_type=MESH,
        )

    def own_copies(r):
        recv = kv_recv.at[r, b]
        return [
            pass_on(piece(r, b), own_send.at[r, n], recv, blk)
            for n, blk in enumerate((up, down, sibling))
        ]

    def relay_copies(r):
        return [
            [
                pass_on(kvbuf.at[r, 0, down], relay_send.at[r, 0], kv_recv.at[r, down], up),
                pass_on(piece(r, down), relay_send.at[r, 1], kv_recv.at[r, down], sibling),
            ],
            [
                pass_on(kvbuf.at[r, 1, up], relay_send.at[r, 2], kv_recv.at[r, up], down),
                pass_on(piece(r, up), relay_send.at[r, 3], kv_recv.at[r, up], sibling),
            ],
        ]

    def opp_copy(r):
        return pass_on(piece(r, across), opp_send.at[r], kv_recv.at[r, across], sibling)

    def compute(r):
        source = lax.rem(z + offset_of(r) + 8, 8)
        rows = lax.broadcasted_iota(jnp.int32, (HEAD, HEAD), 0)
        cols = lax.broadcasted_iota(jnp.int32, (HEAD, HEAD), 1)
        allowed = cols + (source - home) * HEAD <= rows
        for n in range(8):
            keys = kvbuf[r, 0, : n + 1].reshape((n + 1) * HEAD, HEAD)
            values = kvbuf[r, 1, : n + 1].reshape((n + 1) * HEAD, HEAD)
            scores = lax.dot_general(
                qbuf[n], keys, (((1,), (1,)), ((), ())), preferred_element_type=jnp.float32
            )
            last = jnp.where(allowed, scores[:, n * HEAD :], MASKED)
            if n:
                scores = jnp.concatenate([scores[:, : n * HEAD], last], 1)
            else:
                scores = last
            before = maxima[n]
            highest = jnp.maximum(before, scores.max(-1, keepdims=True) * SCALE)
            weights = jnp.exp2(scores * SCALE - jnp.concatenate([highest] * (n + 1), 1))
            factor = jnp.exp2(before - highest)
            extended = jnp.concatenate([values, jnp.ones_like(values)], 1)
            summed = jnp.dot(
                weights.astype(jnp.bfloat16), extended, preferred_element_type=jnp.float32
            )
            acc[n] = acc[n] * jnp.concatenate([factor, factor], 1) + summed
            maxima[n] = highest

    def o_copy(n):
        return pltpu.make_async_remote_copy(
            src_ref=obuf.at[n],
            dst_ref=abuf.at[:, head_columns(z)],
            send_sem=o_send.at[n],
            recv_sem=o_recv,
            device_id={"blk": n, "wide": home},
            device_id_type=MESH,
        )

    def o_local(n):
        return pltpu.make_async_copy(obuf.at[n], abuf.at[:, head_columns(z)], o_recv)

    def pool_target():
        return ph.at[pl.ds(pl.multiple_of(home * 32, 32), 32)]

    def pool_copy(n):
        return remote(
            pobuf.at[n], pool_target(), po_send.at[n], ph_recv, {"blk": n, "wide": z}
        )

    def pool_local(n):
        return pltpu.make_async_copy(pobuf.at[n], pool_target(), ph_recv)

    def edge_copy(n):
        return remote(
            pobuf.at[n, pl.ds(16, 16)],
            ph.at[pl.ds(256, 16)],
            px_send.at[n],
            px_recv,
            {"blk": n + 1, "wide": z},
        )

    def edge_local(n):
        return pltpu.make_async_copy(pobuf.at[n, pl.ds(16, 16)], ph.at[pl.ds(256, 16)], px_recv)

    def spread_copy(j):
        where = {"blk": b, "wide": lax.rem(z + j, 8)}
        return remote(poh, pst.at[:, head_columns(z)], pg_send.at[j - 1], po_recv, where)

    def spread_local():
        return pltpu.make_async_copy(poh, pst.at[:, head_columns(z)], po_recv)

    @pl.when(z < FINE_HEADS)
    def _():
        @pl.loop(0, ROUNDS + LAST)
        def _(i):
            def stage(late):
                return jnp.logical_and(i >= late, i < ROUNDS + late)

            @pl.when(i < ROUNDS)
            def _():
                landed(piece(i, b), kv_recv.at[i, b])

                @pl.when(jnp.logical_and(i > 0, i < ROUNDS - LEAD))
                def _():
                    send_round(i + LEAD)

                for copy in own_copies(i):
                    copy.start()

            @pl.when(stage(RELAY))
            def _():
                r = i - RELAY
                first, second = relay_copies(r)
                landed(piece(r, down), kv_recv.at[r, down])
                for copy in first:
                    copy.start()
                landed(piece(r, up), kv_recv.at[r, up])
                for copy in second:
                    copy.start()

            @pl.when(stage(ACROSS))
            def _():
                r = i - ACROSS
                landed(piece(r, across), kv_recv.at[r, across])
                opp_copy(r).start()

            @pl.when(i == GRADS)
            def _():
                send_grads()

            @pl.when(i == LAST)
            def _():
                for n in range(8):
                    landed(qbuf.at[n], q_recv.at[n])

            @pl.when(i >= LAST)
            def _():
                r = i - LAST
                for n in range(4):
                    other = lax.rem(sibling + 2 * n, 8)
                    landed(piece(r, other), kv_recv.at[r, other])
                compute(r)

        short = lax.broadcasted_iota(jnp.int32, (32, HEAD), 0)
        inside = lax.broadcasted_iota(jnp.int32, (32, HEAD), 1) - 8 * short
        taken = jnp.where(
            short < 16,
            jnp.logical_and(inside >= -1, inside < 7).astype(jnp.int32),
            jnp.logical_and(short == 16, inside == -1).astype(jnp.int32),
        )
        pool = jnp.where(taken == 1, 0.125, 0.0).astype(jnp.bfloat16)
        for n in range(8):
            total = acc[n]
            out = (total[:, :HEAD] / total[:, HEAD:]).astype(jnp.bfloat16)
            obuf[n] = out
            pobuf[n] = jnp.dot(pool, out, preferred_element_type=jnp.float32).astype(jnp.bfloat16)

            @pl.when(n == b)
            def _():
                pool_local(n).start()

            @pl.when(n != b)
            def _():
                pool_copy(n).start()

            if n < 7:

                @pl.when(jnp.logical_and(home == 7, n + 1 == b))
                def _():
                    edge_local(n).start()

                @pl.when(jnp.logical_and(home == 7, n + 1 != b))
                def _():
                    edge_copy(n).start()

        row = lax.broadcasted_iota(jnp.int32, (128, 272), 0)
        col = lax.broadcasted_iota(jnp.int32, (128, 272), 1)
        group = lax.shift_right_logical(row, 4)
        within = jnp.bitwise_and(row, 15)
        edge = jnp.where(group == 0, 256, 32 * group - 16)
        picked = jnp.logical_or(
            col == 32 * group + within, jnp.logical_and(within == 0, col == edge)
        )
        picked = jnp.where(picked, 1.0, 0.0).astype(jnp.bfloat16)

        @pl.when(b > 0)
        def _():
            landed(ph.at[pl.ds(256, 16)], px_recv)

        landed(ph.at[pl.ds(0, 256)], ph_recv)
        poh[...] = jnp.dot(picked, ph[...], preferred_element_type=jnp.float32).astype(jnp.bfloat16)
        spread_local().start()

        @pl.loop(1, 8)
        def _(j):
            spread_copy(j).start()

        for n in range(8):
            here = jnp.logical_and(n == b, z == home)

            @pl.when(here)
            def _():
                o_local(n).start()

            @pl.when(jnp.logical_not(here))
            def _():
                o_copy(n).start()

    landed(gw.at[pl.ds(0, 112)], gw_recv)
    def same_core(j):
        return remote(
            ab.at[b],
            ab.at[b],
            ab_send.at[j - 1],
            ab_recv.at[b],
            {"blk": lax.rem(b + 2 * j, 8), "wide": z},
        )

    def share(slot, n):
        return remote(
            ab.at[slot], ab.at[slot], sib_send.at[n], ab_recv.at[slot], {"blk": sibling, "wide": z}
        )

    def window(ref, to):
        return ref.at[:, pl.ds(pl.multiple_of(to * 192 // 128 * 128, 128), 256)]

    def window_copy(src, dst, send, recv, j):
        to = lax.rem(b + j, 8)
        return remote(
            window(src, to), dst.at[b], send.at[j - 1], recv, {"blk": to, "wide": z}
        )

    kept = [
        pltpu.make_async_copy(window(nbuf, b), nwin.at[b], nwin_send.at[7]),
        pltpu.make_async_copy(window(gw, b), gwin.at[b], gwin_send.at[7]),
    ]
    kept[1].start()

    @pl.loop(1, 8)
    def _(j):
        window_copy(gw, gwin, gwin_send, gwin_recv, j).start()

    for copy in weights_in:
        copy.wait()
    act_grad = lax.dot_general(
        gw[...], w2_ref[...], (((1,), (1,)), ((), ())), preferred_element_type=jnp.float32
    )

    landed(cw.at[pl.ds(0, 7)], cw_recv)
    counts = cw[...].reshape(128, 128)[:, :VOCAB].astype(jnp.float32)
    embedded = jnp.dot(
        counts,
        emb_ref[...],
        precision=lax.Precision.HIGHEST,
        preferred_element_type=jnp.float32,
    )
    landed(pst, po_recv)
    pooled = embedded + jnp.dot(pst[...], mixer_ref[...], preferred_element_type=jnp.float32)
    pooled = pooled.astype(jnp.bfloat16)
    pw[...] = pooled
    pooled_wide = pooled.astype(jnp.float32)
    scale = lax.rsqrt(jnp.mean(pooled_wide * pooled_wide, -1, keepdims=True) + 1e-06)
    normed = (pooled_wide * scale).astype(jnp.bfloat16)
    nbuf[...] = normed
    expanded = jnp.dot(normed, w1_ref[...], preferred_element_type=jnp.float32)
    activated, slope = gelu_parts(expanded)
    activated = activated.astype(jnp.bfloat16)
    pbuf[...] = jnp.dot(
        activated, w2_ref[...], preferred_element_type=jnp.float32
    ).astype(jnp.bfloat16)

    def sum_copy(j):
        to = lax.rem(z + j, 8)
        return remote(
            pbuf.at[pl.ds(pl.multiple_of(to * 16, 16), 16)],
            rsb.at[j - 1],
            rs_send.at[j - 1],
            rs_recv,
            {"blk": b, "wide": to},
        )

    @pl.loop(1, 8)
    def _(j):
        sum_copy(j).start()

    ab[b, :, :384] = activated
    ab[b, :, 384:] = (act_grad * slope).astype(jnp.bfloat16)

    @pl.loop(1, 4)
    def _(j):
        same_core(j).start()

    share(b, 0).start()
    kept[0].start()

    @pl.loop(1, 8)
    def _(j):
        window_copy(nbuf, nwin, nwin_send, nwin_recv, j).start()

    kind = lax.broadcasted_iota(jnp.int32, (VOCAB, 128), 0)
    onehot = (kind == tok_ref[...]).astype(jnp.float32)
    stream = lax.dot_general(
        onehot,
        emb_ref[...],
        (((0,), (0,)), ((), ())),
        precision=lax.Precision.HIGHEST,
        preferred_element_type=jnp.float32,
    )
    landed(abuf, o_recv)
    sbuf[...] = stream + jnp.dot(
        abuf[...], mixer_ref[...], preferred_element_type=jnp.float32
    )

    landed(rsb, rs_recv)
    middle = pw[mine, :].astype(jnp.float32) + pbuf[mine, :].astype(jnp.float32)
    for n in range(7):
        middle = middle + rsb[n].astype(jnp.float32)
    mbuf[8:] = middle
    row_out[1] = middle[15:]

    @pl.when(not_last)
    def _():
        row_copy(1, following).start()

    for j in range(1, 4):
        slot = lax.rem(b + 2 * j, 8)
        landed(ab.at[slot], ab_recv.at[slot])
        share(slot, j).start()

    @pl.when(not_first)
    def _():
        landed(row_in.at[1], row_recv.at[1])

    mbuf[:8] = at_row(7, row_in[1])
    steps = lax.broadcasted_iota(jnp.int32, (8, 1536), 0).astype(jnp.float32)
    ahead, behind = (steps + 1.0) / 8, (7.0 - steps) / 8
    for j in range(0, 16, 2):
        rows = [
            sbuf[8 * n : 8 * (n + 1)]
            + mbuf[8 + n : 9 + n] * ahead
            + mbuf[7 + n : 8 + n] * behind
            for n in (j, j + 1)
        ]
        restored_ref[8 * j : 8 * (j + 2)] = jnp.concatenate(rows, 0).astype(jnp.bfloat16)

    for n in range(4):
        slot = lax.rem(sibling + 2 * n, 8)
        landed(ab.at[slot], ab_recv.at[slot])
    landed(nwin.at[pl.ds(0, 7)], nwin_recv)
    landed(gwin.at[pl.ds(0, 7)], gwin_recv)
    for copy in kept:
        copy.wait()
    tokens = (((0,), (0,)), ((), ()))
    both = ab[...].reshape(1024, 768)
    expanded = lax.dot_general(
        nwin[...].reshape(1024, 256), both[:, 384:], tokens, preferred_element_type=jnp.float32
    )
    odd = lax.rem(b, 2)
    reduced = lax.dot_general(
        gwin[...].reshape(1024, 256), both[:, :384], tokens, preferred_element_type=jnp.float32
    )

    @pl.when(odd == 0)
    def _():
        expand_ref[...] = expanded[:192]
        reduce_ref[...] = reduced[:192]

    @pl.when(odd == 1)
    def _():
        expand_ref[...] = expanded[64:]
        reduce_ref[...] = reduced[64:]

    @pl.when(holds_head)
    def _():
        @pl.loop(0, ROUNDS)
        def _(r):
            for copy in own_copies(r):
                copy.wait_send()
            for pair in relay_copies(r):
                for copy in pair:
                    copy.wait_send()
            opp_copy(r).wait_send()

        @pl.loop(1, ROUNDS)
        def _(r):
            wait_round(r)

        @pl.loop(0, 8)
        def _(n):
            @pl.when(jnp.logical_not(jnp.logical_and(n == b, z == home)))
            def _():
                o_copy(n).wait_send()

            @pl.when(n != b)
            def _():
                pool_copy(n).wait_send()

            @pl.when(jnp.logical_and(jnp.logical_and(home == 7, n < 7), n + 1 != b))
            def _():
                edge_copy(n).wait_send()

        @pl.loop(1, 8)
        def _(j):
            spread_copy(j).wait_send()

    @pl.loop(0, FINE_HEADS)
    def _(h):
        @pl.when(jnp.logical_not(is_self(h)))
        def _():
            q_copy(h).wait_send()

    @pl.when(not_last)
    def _():
        row_copy(1, following).wait_send()
        tok_copy().wait_send()

    @pl.when(not_first)
    def _():
        row_copy(0, preceding).wait_send()

    @pl.loop(1, 8)
    def _(j):
        count_copy(j).wait_send()
        wide_copy(gw, gw_send, gw_recv, j).wait_send()
        sum_copy(j).wait_send()
        window_copy(nbuf, nwin, nwin_send, nwin_recv, j).wait_send()
        window_copy(gw, gwin, gwin_send, gwin_recv, j).wait_send()

    @pl.loop(1, 4)
    def _(j):
        same_core(j).wait_send()

    share(b, 0).wait_send()
    for j in range(1, 4):
        share(lax.rem(b + 2 * j, 8), j).wait_send()


def whole_step(*arrays):
    rows = 128
    vmem = pl.BlockSpec(memory_space=pltpu.VMEM)
    hbm = pl.BlockSpec(memory_space=pl.ANY)
    dma = pltpu.SemaphoreType.DMA
    f32, bf16 = jnp.float32, jnp.bfloat16
    return pl.pallas_call(
        step_kernel,
        name="step",
        out_shape=(
            jax.ShapeDtypeStruct((rows, 1536), bf16),
            jax.ShapeDtypeStruct((192, 384), f32),
            jax.ShapeDtypeStruct((192, 384), f32),
        ),
        in_specs=[vmem] * 2 + [hbm] * 7,
        out_specs=(vmem,) * 3,
        scratch_shapes=[
            pltpu.VMEM((rows, 768), bf16),
            pltpu.VMEM((rows, 768), bf16),
            pltpu.VMEM((rows, 768), bf16),
            pltpu.VMEM((rows, 1536), bf16),
            pltpu.VMEM((8, rows, HEAD), bf16),
            pltpu.VMEM((ROUNDS, 2, 8, rows, HEAD), bf16),
            pltpu.VMEM((8, rows, 2 * HEAD), f32),
            pltpu.VMEM((8, rows, HEAD), f32),
            pltpu.VMEM((8, rows, HEAD), bf16),
            pltpu.VMEM((8, 32, HEAD), bf16),
            pltpu.VMEM((rows, 768), bf16),
            pltpu.VMEM((rows, 768), bf16),
            pltpu.VMEM((272, HEAD), bf16),
            pltpu.VMEM((rows, HEAD), bf16),
            pltpu.VMEM((768, 1536), bf16),
            pltpu.VMEM((1536, 384), bf16),
            pltpu.VMEM((384, 1536), bf16),
            pltpu.VMEM((24, 1536), f32),
            pltpu.VMEM((16, 1536), f32),
            pltpu.VMEM((24, 1536), f32),
            pltpu.VMEM((2, 1, 1536), f32),
            pltpu.VMEM((2, 1, 1536), f32),
            pltpu.VMEM((1, 128), jnp.int32),
            pltpu.VMEM((8, 16, 128), bf16),
            pltpu.VMEM((128, 1536), bf16),
            pltpu.VMEM((128, 1536), bf16),
            pltpu.VMEM((128, 1536), bf16),
            pltpu.VMEM((128, 1536), bf16),
            pltpu.VMEM((7, 16, 1536), bf16),
            pltpu.VMEM((8, 128, 768), bf16),
            pltpu.VMEM((8, 128, 256), bf16),
            pltpu.VMEM((8, 128, 256), bf16),
            pltpu.VMEM((128, 1536), f32),
            pltpu.SemaphoreType.REGULAR,
            dma((7,)),
            dma((FINE_HEADS,)),
            dma((ROUNDS, 2)),
            dma((ROUNDS, 3)),
            dma((ROUNDS, 4)),
            dma((ROUNDS,)),
            dma((8,)),
            dma((8,)),
            dma((8,)),
            dma((7,)),
            dma((8,)),
            dma((ROUNDS, 8)),
            dma,
            dma,
            dma,
            dma,
            dma((2,)),
            dma((2,)),
            dma,
            dma,
            dma((7,)),
            dma,
            dma((7,)),
            dma((7,)),
            dma((3,)),
            dma((4,)),
            dma((8,)),
            dma((8,)),
            dma,
            dma,
            dma((8,)),
            dma,
            dma,
        ],
        compiler_params=pltpu.CompilerParams(collective_id=0, has_side_effects=True),
    )(*arrays)


def local(
    token_ids,
    embedding,
    queries,
    key_rows,
    value_rows,
    head_mixer,
    expand_weight,
    reduce_weight,
    cotangent,
):
    restored, expand_grad, reduce_grad = whole_step(
        token_ids.reshape(1, -1),
        embedding,
        queries,
        key_rows,
        value_rows,
        cotangent,
        head_mixer,
        expand_weight,
        reduce_weight,
    )
    return restored, expand_grad, reduce_grad.T


def solution(mesh):
    return jax.shard_map(
        local,
        mesh=mesh,
        in_specs=(
            P(("dp", "blk", "wide")),
            P(),
            P(("dp", "blk", "wide"), None),
            P(("dp", "blk", "wide"), None),
            P(("dp", "blk", "wide"), None),
            P(),
            P(None, "wide"),
            P("wide", None),
            P(("dp", "blk", "wide"), None),
        ),
        out_specs=(
            P(("dp", "blk", "wide"), None),
            P(("dp", "blk"), "wide"),
            P(("dp", "wide"), "blk"),
        ),
        check_vma=False,
    )
```

```python
import jax
import jax.numpy as jnp
from jax import lax
from jax.experimental import pallas as pl
from jax.experimental.pallas import tpu as pltpu
from jax.sharding import PartitionSpec as P

FINE_HEADS = 6
HEAD = 128
VOCAB = 6


MESH = pl.DeviceIdType.MESH
ROUNDS = 8
RELAY, ACROSS, LAST = 2, 4, 5
LEAD = 3
GRADS = 5
SCALE = HEAD ** (-0.5) * 1.4426950408889634
MASKED = -2e38
EMPTY = -1e30


def offset_of(r):
    return (r + 1) // 2 * (2 * (r % 2) - 1)


def landed(ref, sem):
    pltpu.make_async_copy(ref, ref, sem).wait()


def gelu_parts(x):
    root = 0.7978845608028654
    inner = jnp.tanh(root * (x + 0.044715 * x * x * x))
    slope = 0.5 * (1.0 + inner) + 0.5 * x * (1.0 - inner * inner) * root * (
        1.0 + 3 * 0.044715 * x * x
    )
    return 0.5 * x * (1.0 + inner), slope


def step_kernel(
    tok_ref,
    emb_ref,
    q_hbm,
    k_hbm,
    v_hbm,
    cot_hbm,
    mixer_hbm,
    w1_hbm,
    w2_hbm,
    restored_ref,
    expand_ref,
    reduce_ref,
    q_ref,
    k_ref,
    v_ref,
    cot_ref,
    qbuf,
    kvbuf,
    acc,
    maxima,
    obuf,
    pobuf,
    abuf,
    pst,
    ph,
    poh,
    mixer_ref,
    w1_ref,
    w2_ref,
    lbuf,
    obuf16,
    mbuf,
    row_out,
    row_in,
    tok_in,
    cw,
    pw,
    gw,
    nbuf,
    pbuf,
    rsb,
    ab,
    nwin,
    gwin,
    sbuf,
    ready,
    w_sem,
    q_send,
    kv_send,
    own_send,
    relay_send,
    opp_send,
    o_send,
    po_send,
    px_send,
    pg_send,
    q_recv,
    kv_recv,
    o_recv,
    po_recv,
    ph_recv,
    px_recv,
    row_send,
    row_recv,
    tok_send,
    tok_recv,
    cw_send,
    cw_recv,
    gw_send,
    rs_send,
    ab_send,
    sib_send,
    nwin_send,
    gwin_send,
    gw_recv,
    rs_recv,
    ab_recv,
    nwin_recv,
    gwin_recv,
):
    b = lax.axis_index("blk")
    z = lax.axis_index("wide")
    place = b * 8 + z
    sibling = b + 1 - 2 * lax.rem(b, 2)
    up = lax.rem(b + 2, 8)
    down = lax.rem(b + 6, 8)
    across = lax.rem(b + 4, 8)
    home = lax.rem(b + 3 * z, 8)
    holds_head = z < FINE_HEADS
    first, last = place == 0, place == 63
    not_first, not_last = place > 0, place < 63
    following = {"blk": lax.rem(b + (z + 1) // 8, 8), "wide": lax.rem(z + 1, 8)}
    preceding = {"blk": lax.rem(b + 8 - (8 - z) // 8, 8), "wide": lax.rem(z + 7, 8)}

    def holder(wide, h):
        return lax.rem(wide + 5 * h, 8)

    barrier = pltpu.get_barrier_semaphore()

    def greet(sem, where):
        pl.semaphore_signal(sem, inc=1, device_id=where, device_id_type=MESH)

    @pl.loop(1, 8)
    def _(j):
        greet(barrier, {"blk": b, "wide": lax.rem(z + j, 8)})
        greet(barrier, {"blk": lax.rem(b + j, 8), "wide": z})

    weights_in = [
        pltpu.make_async_copy(src, dst, w_sem.at[n])
        for n, (src, dst) in enumerate(
            ((mixer_hbm, mixer_ref), (w1_hbm, w1_ref), (w2_hbm, w2_ref))
        )
    ]
    rows_in = [
        pltpu.make_async_copy(src, dst, w_sem.at[n + 3])
        for n, (src, dst) in enumerate(
            ((k_hbm, k_ref), (v_hbm, v_ref), (q_hbm, q_ref), (cot_hbm, cot_ref))
        )
    ]
    for copy in rows_in:
        copy.start()

    def remote(src, dst, send, recv, where):
        return pltpu.make_async_remote_copy(
            src_ref=src,
            dst_ref=dst,
            send_sem=send,
            recv_sem=recv,
            device_id=where,
            device_id_type=MESH,
        )

    eight = lax.broadcasted_iota(jnp.int32, (8, 1536), 0)

    def at_row(n, row):
        return jnp.where(eight == n, jnp.broadcast_to(row, (8, 1536)), 0.0)

    def row_copy(n, where):
        return remote(row_out.at[n], row_in.at[n], row_send.at[n], row_recv.at[n], where)

    def tok_copy():
        return remote(tok_ref, tok_in, tok_send, tok_recv, following)

    short = lax.broadcasted_iota(jnp.int32, (16, 128), 0)
    inside = lax.broadcasted_iota(jnp.int32, (16, 128), 1) - 8 * short
    own = jnp.logical_and(inside >= 0, inside < 8)
    inside = inside.astype(jnp.float32)
    after = jnp.where(own, (inside + 1.0) / 8, 0.0).astype(jnp.bfloat16)
    before = jnp.where(own, (7.0 - inside) / 8, 0.0).astype(jnp.bfloat16)
    rows_in[3].wait()
    cot = cot_ref[...]
    later_part = jnp.dot(before, cot, preferred_element_type=jnp.float32)
    lbuf[:16] = later_part
    row_out[0] = later_part[:1]
    obuf16[...] = jnp.dot(after, cot, preferred_element_type=jnp.float32)
    acc[...] = jnp.zeros_like(acc)
    maxima[...] = jnp.full_like(maxima, EMPTY)

    @pl.when(last)
    def _():
        row_in[0] = jnp.zeros((1, 1536), jnp.float32)

    @pl.when(first)
    def _():
        row_in[1] = jnp.zeros((1, 1536), jnp.float32)
        tok_in[...] = jnp.full((1, 128), -1, jnp.int32)

    @pl.when(b == 0)
    def _():
        ph[256:] = jnp.zeros((16, HEAD), jnp.bfloat16)

    for copy in rows_in[:3]:
        copy.wait()
    pl.semaphore_wait(barrier, 14)
    mine = pl.ds(pl.multiple_of(z * 16, 16), 16)

    def wide_copy(buf, send, recv, j):
        where = {"blk": b, "wide": lax.rem(z + j, 8)}
        return remote(buf.at[mine], buf.at[mine], send.at[j - 1], recv, where)

    def count_copy(j):
        where = {"blk": b, "wide": lax.rem(z + j, 8)}
        return remote(cw.at[z], cw.at[z], cw_send.at[j - 1], cw_recv, where)

    def send_grads():
        @pl.when(not_last)
        def _():
            landed(row_in.at[0], row_recv.at[0])

        lbuf[16:] = at_row(0, row_in[0])
        gw[mine, :] = (obuf16[...] + lbuf[1:17]).astype(jnp.bfloat16)

        @pl.loop(1, 8)
        def _(j):
            wide_copy(gw, gw_send, gw_recv, j).start()

        @pl.when(not_first)
        def _():
            landed(tok_in, tok_recv)

        lane = lax.broadcasted_iota(jnp.int32, (128, 128), 1)
        kind = lax.broadcasted_iota(jnp.int32, (128, 128), 0)
        shifted = jnp.where(
            lane == 0,
            pltpu.roll(jnp.broadcast_to(tok_in[...], (128, 128)), 1, 1),
            pltpu.roll(jnp.broadcast_to(tok_ref[...], (128, 128)), 1, 1),
        )
        short = lax.broadcasted_iota(jnp.int32, (16, 128), 0)
        inside = lax.broadcasted_iota(jnp.int32, (16, 128), 1) - 8 * short
        eighth = jnp.where(jnp.logical_and(inside >= 0, inside < 8), 0.125, 0.0)
        cw[z] = lax.dot_general(
            eighth.astype(jnp.bfloat16),
            jnp.where(kind == shifted, 1.0, 0.0).astype(jnp.bfloat16),
            (((1,), (1,)), ((), ())),
            preferred_element_type=jnp.float32,
        ).astype(jnp.bfloat16)

        @pl.loop(1, 8)
        def _(j):
            count_copy(j).start()

    def head_columns(h):
        return pl.ds(pl.multiple_of(h * HEAD, HEAD), HEAD)

    def kv_copies(r, h):
        copies = []
        for n, ref in enumerate((k_ref, v_ref)):
            copies.append(
                pltpu.make_async_remote_copy(
                    src_ref=ref.at[:, head_columns(h)],
                    dst_ref=kvbuf.at[r, n, b],
                    send_sem=kv_send.at[r, n],
                    recv_sem=kv_recv.at[r, b],
                    device_id={"blk": b, "wide": h},
                    device_id_type=MESH,
                )
            )
        return copies

    def q_copy(h):
        return pltpu.make_async_remote_copy(
            src_ref=q_ref.at[:, head_columns(h)],
            dst_ref=qbuf.at[b],
            send_sem=q_send.at[h],
            recv_sem=q_recv.at[b],
            device_id={"blk": holder(z, h), "wide": h},
            device_id_type=MESH,
        )

    def q_local():
        return pltpu.make_async_copy(q_ref.at[:, head_columns(z)], qbuf.at[b], q_recv.at[b])

    def is_self(h):
        return jnp.logical_and(z == home, h == z)

    @pl.when(z < FINE_HEADS)
    def _():
        for n, ref in enumerate((k_ref, v_ref)):
            pltpu.make_async_copy(
                ref.at[:, head_columns(z)], kvbuf.at[0, n, b], kv_recv.at[0, b]
            ).start()

    def send_round(r):
        h = lax.rem(z - offset_of(r) + 8, 8)

        @pl.when(h < FINE_HEADS)
        def _():
            for copy in kv_copies(r, h):
                copy.start()

    def wait_round(r):
        h = lax.rem(z - offset_of(r) + 8, 8)

        @pl.when(h < FINE_HEADS)
        def _():
            for copy in kv_copies(r, h):
                copy.wait_send()

    for r in range(1, LEAD + 1):
        send_round(r)

    def send_queries():
        @pl.loop(0, FINE_HEADS)
        def _(h):
            @pl.when(is_self(h))
            def _():
                q_local().start()

            @pl.when(jnp.logical_not(is_self(h)))
            def _():
                q_copy(h).start()

    @pl.loop(1, 8)
    def _(j):
        greet(ready, {"blk": lax.rem(b + j, 8), "wide": z})

    for copy in weights_in:
        copy.start()
    pl.semaphore_wait(ready, 7)
    send_queries()

    @pl.when(not_last)
    def _():
        tok_copy().start()

    @pl.when(not_first)
    def _():
        row_copy(0, preceding).start()

    @pl.when(jnp.logical_not(holds_head))
    def _():
        @pl.loop(1, ROUNDS)
        def _(r):
            wait_round(r)

            @pl.when(r < ROUNDS - LEAD)
            def _():
                send_round(r + LEAD)

        send_grads()

    def piece(r, blk):
        return kvbuf.at[r, :, blk]

    def pass_on(src, sem, recv, blk):
        return pltpu.make_async_remote_copy(
            src_ref=src,
            dst_ref=src,
            send_sem=sem,
            recv_sem=recv,
            device_id={"blk": blk, "wide": z},
            device_id_type=MESH,
        )

    def own_copies(r):
        recv = kv_recv.at[r, b]
        return [
            pass_on(piece(r, b), own_send.at[r, n], recv, blk)
            for n, blk in enumerate((up, down, sibling))
        ]

    def relay_copies(r):
        return [
            [
                pass_on(kvbuf.at[r, 0, down], relay_send.at[r, 0], kv_recv.at[r, down], up),
                pass_on(piece(r, down), relay_send.at[r, 1], kv_recv.at[r, down], sibling),
            ],
            [
                pass_on(kvbuf.at[r, 1, up], relay_send.at[r, 2], kv_recv.at[r, up], down),
                pass_on(piece(r, up), relay_send.at[r, 3], kv_recv.at[r, up], sibling),
            ],
        ]

    def opp_copy(r):
        return pass_on(piece(r, across), opp_send.at[r], kv_recv.at[r, across], sibling)

    def compute(r):
        source = lax.rem(z + offset_of(r) + 8, 8)
        pair = 2 * HEAD
        row = lax.broadcasted_iota(jnp.int32, (pair, pair), 0)
        col = lax.broadcasted_iota(jnp.int32, (pair, pair), 1)
        gap = col - row + 7 * HEAD * (
            lax.shift_right_logical(col, 7) - lax.shift_right_logical(row, 7)
        )
        allowed = gap + (source - home) * HEAD <= 0
        for n in range(0, 8, 2):
            m = n + 2
            keys = kvbuf[r, 0, :m].reshape(m * HEAD, HEAD)
            values = kvbuf[r, 1, :m].reshape(m * HEAD, HEAD)
            scores = lax.dot_general(
                qbuf[n:m].reshape(pair, HEAD),
                keys,
                (((1,), (1,)), ((), ())),
                preferred_element_type=jnp.float32,
            )
            last = jnp.where(allowed, scores[:, n * HEAD :], MASKED)
            if n:
                scores = jnp.concatenate([scores[:, : n * HEAD], last], 1)
            else:
                scores = last
            before = maxima[n:m].reshape(pair, HEAD)
            highest = jnp.maximum(before, scores.max(-1, keepdims=True) * SCALE)
            weights = jnp.exp2(scores * SCALE - jnp.concatenate([highest] * m, 1))
            factor = jnp.exp2(before - highest)
            extended = jnp.concatenate([values, jnp.ones_like(values)], 1)
            summed = jnp.dot(
                weights.astype(jnp.bfloat16), extended, preferred_element_type=jnp.float32
            )
            held = acc[n:m].reshape(pair, pair) * jnp.concatenate([factor, factor], 1) + summed
            acc[n:m] = held.reshape(2, HEAD, pair)
            maxima[n:m] = highest.reshape(2, HEAD, HEAD)

    def o_copy(n):
        return pltpu.make_async_remote_copy(
            src_ref=obuf.at[n],
            dst_ref=abuf.at[:, head_columns(z)],
            send_sem=o_send.at[n],
            recv_sem=o_recv,
            device_id={"blk": n, "wide": home},
            device_id_type=MESH,
        )

    def o_local(n):
        return pltpu.make_async_copy(obuf.at[n], abuf.at[:, head_columns(z)], o_recv)

    def pool_target():
        return ph.at[pl.ds(pl.multiple_of(home * 32, 32), 32)]

    def pool_copy(n):
        return remote(
            pobuf.at[n], pool_target(), po_send.at[n], ph_recv, {"blk": n, "wide": z}
        )

    def pool_local(n):
        return pltpu.make_async_copy(pobuf.at[n], pool_target(), ph_recv)

    def edge_copy(n):
        return remote(
            pobuf.at[n, pl.ds(16, 16)],
            ph.at[pl.ds(256, 16)],
            px_send.at[n],
            px_recv,
            {"blk": n + 1, "wide": z},
        )

    def edge_local(n):
        return pltpu.make_async_copy(pobuf.at[n, pl.ds(16, 16)], ph.at[pl.ds(256, 16)], px_recv)

    def spread_copy(j):
        where = {"blk": b, "wide": lax.rem(z + j, 8)}
        return remote(poh, pst.at[:, head_columns(z)], pg_send.at[j - 1], po_recv, where)

    def spread_local():
        return pltpu.make_async_copy(poh, pst.at[:, head_columns(z)], po_recv)

    @pl.when(z < FINE_HEADS)
    def _():
        @pl.loop(0, ROUNDS + LAST)
        def _(i):
            def stage(late):
                return jnp.logical_and(i >= late, i < ROUNDS + late)

            @pl.when(i < ROUNDS)
            def _():
                landed(piece(i, b), kv_recv.at[i, b])

                @pl.when(jnp.logical_and(i > 0, i < ROUNDS - LEAD))
                def _():
                    send_round(i + LEAD)

                for copy in own_copies(i):
                    copy.start()

            @pl.when(stage(RELAY))
            def _():
                r = i - RELAY
                first, second = relay_copies(r)
                landed(piece(r, down), kv_recv.at[r, down])
                for copy in first:
                    copy.start()
                landed(piece(r, up), kv_recv.at[r, up])
                for copy in second:
                    copy.start()

            @pl.when(stage(ACROSS))
            def _():
                r = i - ACROSS
                landed(piece(r, across), kv_recv.at[r, across])
                opp_copy(r).start()

            @pl.when(i == GRADS)
            def _():
                send_grads()

            @pl.when(i == LAST)
            def _():
                for n in range(8):
                    landed(qbuf.at[n], q_recv.at[n])

            @pl.when(i >= LAST)
            def _():
                r = i - LAST
                for n in range(4):
                    other = lax.rem(sibling + 2 * n, 8)
                    landed(piece(r, other), kv_recv.at[r, other])
                compute(r)

        short = lax.broadcasted_iota(jnp.int32, (32, HEAD), 0)
        inside = lax.broadcasted_iota(jnp.int32, (32, HEAD), 1) - 8 * short
        taken = jnp.where(
            short < 16,
            jnp.logical_and(inside >= -1, inside < 7).astype(jnp.int32),
            jnp.logical_and(short == 16, inside == -1).astype(jnp.int32),
        )
        pool = jnp.where(taken == 1, 0.125, 0.0).astype(jnp.bfloat16)
        for n in range(8):
            total = acc[n]
            out = (total[:, :HEAD] / total[:, HEAD:]).astype(jnp.bfloat16)
            obuf[n] = out
            pobuf[n] = jnp.dot(pool, out, preferred_element_type=jnp.float32).astype(jnp.bfloat16)

            @pl.when(n == b)
            def _():
                pool_local(n).start()

            @pl.when(n != b)
            def _():
                pool_copy(n).start()

            if n < 7:

                @pl.when(jnp.logical_and(home == 7, n + 1 == b))
                def _():
                    edge_local(n).start()

                @pl.when(jnp.logical_and(home == 7, n + 1 != b))
                def _():
                    edge_copy(n).start()

        row = lax.broadcasted_iota(jnp.int32, (128, 272), 0)
        col = lax.broadcasted_iota(jnp.int32, (128, 272), 1)
        group = lax.shift_right_logical(row, 4)
        within = jnp.bitwise_and(row, 15)
        edge = jnp.where(group == 0, 256, 32 * group - 16)
        picked = jnp.logical_or(
            col == 32 * group + within, jnp.logical_and(within == 0, col == edge)
        )
        picked = jnp.where(picked, 1.0, 0.0).astype(jnp.bfloat16)

        @pl.when(b > 0)
        def _():
            landed(ph.at[pl.ds(256, 16)], px_recv)

        landed(ph.at[pl.ds(0, 256)], ph_recv)
        poh[...] = jnp.dot(picked, ph[...], preferred_element_type=jnp.float32).astype(jnp.bfloat16)
        spread_local().start()

        @pl.loop(1, 8)
        def _(j):
            spread_copy(j).start()

        for n in range(8):
            here = jnp.logical_and(n == b, z == home)

            @pl.when(here)
            def _():
                o_local(n).start()

            @pl.when(jnp.logical_not(here))
            def _():
                o_copy(n).start()

    landed(gw.at[pl.ds(0, 112)], gw_recv)
    def same_core(j):
        return remote(
            ab.at[b],
            ab.at[b],
            ab_send.at[j - 1],
            ab_recv.at[b],
            {"blk": lax.rem(b + 2 * j, 8), "wide": z},
        )

    def share(slot, n):
        return remote(
            ab.at[slot], ab.at[slot], sib_send.at[n], ab_recv.at[slot], {"blk": sibling, "wide": z}
        )

    def window(ref, to):
        return ref.at[:, pl.ds(pl.multiple_of(to * 192 // 128 * 128, 128), 256)]

    def window_copy(src, dst, send, recv, j):
        to = lax.rem(b + j, 8)
        return remote(
            window(src, to), dst.at[b], send.at[j - 1], recv, {"blk": to, "wide": z}
        )

    kept = [
        pltpu.make_async_copy(window(nbuf, b), nwin.at[b], nwin_send.at[7]),
        pltpu.make_async_copy(window(gw, b), gwin.at[b], gwin_send.at[7]),
    ]
    kept[1].start()

    @pl.loop(1, 8)
    def _(j):
        window_copy(gw, gwin, gwin_send, gwin_recv, j).start()

    for copy in weights_in:
        copy.wait()
    act_grad = lax.dot_general(
        gw[...], w2_ref[...], (((1,), (1,)), ((), ())), preferred_element_type=jnp.float32
    )

    landed(cw.at[pl.ds(0, 7)], cw_recv)
    counts = cw[...].reshape(128, 128)[:, :VOCAB].astype(jnp.float32)
    embedded = jnp.dot(
        counts,
        emb_ref[...],
        precision=lax.Precision.HIGHEST,
        preferred_element_type=jnp.float32,
    )
    landed(pst, po_recv)
    pooled = embedded + jnp.dot(pst[...], mixer_ref[...], preferred_element_type=jnp.float32)
    pooled = pooled.astype(jnp.bfloat16)
    pw[...] = pooled
    pooled_wide = pooled.astype(jnp.float32)
    scale = lax.rsqrt(jnp.mean(pooled_wide * pooled_wide, -1, keepdims=True) + 1e-06)
    normed = (pooled_wide * scale).astype(jnp.bfloat16)
    nbuf[...] = normed
    expanded = jnp.dot(normed, w1_ref[...], preferred_element_type=jnp.float32)
    activated, slope = gelu_parts(expanded)
    activated = activated.astype(jnp.bfloat16)
    pbuf[...] = jnp.dot(
        activated, w2_ref[...], preferred_element_type=jnp.float32
    ).astype(jnp.bfloat16)

    def sum_copy(j):
        to = lax.rem(z + j, 8)
        return remote(
            pbuf.at[pl.ds(pl.multiple_of(to * 16, 16), 16)],
            rsb.at[j - 1],
            rs_send.at[j - 1],
            rs_recv,
            {"blk": b, "wide": to},
        )

    @pl.loop(1, 8)
    def _(j):
        sum_copy(j).start()

    ab[b, :, :384] = activated
    ab[b, :, 384:] = (act_grad * slope).astype(jnp.bfloat16)

    @pl.loop(1, 4)
    def _(j):
        same_core(j).start()

    share(b, 0).start()
    kept[0].start()

    @pl.loop(1, 8)
    def _(j):
        window_copy(nbuf, nwin, nwin_send, nwin_recv, j).start()

    kind = lax.broadcasted_iota(jnp.int32, (VOCAB, 128), 0)
    onehot = (kind == tok_ref[...]).astype(jnp.float32)
    stream = lax.dot_general(
        onehot,
        emb_ref[...],
        (((0,), (0,)), ((), ())),
        precision=lax.Precision.HIGHEST,
        preferred_element_type=jnp.float32,
    )
    landed(abuf, o_recv)
    sbuf[...] = stream + jnp.dot(
        abuf[...], mixer_ref[...], preferred_element_type=jnp.float32
    )

    landed(rsb, rs_recv)
    middle = pw[mine, :].astype(jnp.float32) + pbuf[mine, :].astype(jnp.float32)
    for n in range(7):
        middle = middle + rsb[n].astype(jnp.float32)
    mbuf[8:] = middle
    row_out[1] = middle[15:]

    @pl.when(not_last)
    def _():
        row_copy(1, following).start()

    for j in range(1, 4):
        slot = lax.rem(b + 2 * j, 8)
        landed(ab.at[slot], ab_recv.at[slot])
        share(slot, j).start()

    @pl.when(not_first)
    def _():
        landed(row_in.at[1], row_recv.at[1])

    mbuf[:8] = at_row(7, row_in[1])
    steps = lax.broadcasted_iota(jnp.int32, (8, 1536), 0).astype(jnp.float32)
    ahead, behind = (steps + 1.0) / 8, (7.0 - steps) / 8
    for j in range(0, 16, 2):
        rows = [
            sbuf[8 * n : 8 * (n + 1)]
            + mbuf[8 + n : 9 + n] * ahead
            + mbuf[7 + n : 8 + n] * behind
            for n in (j, j + 1)
        ]
        restored_ref[8 * j : 8 * (j + 2)] = jnp.concatenate(rows, 0).astype(jnp.bfloat16)

    for n in range(4):
        slot = lax.rem(sibling + 2 * n, 8)
        landed(ab.at[slot], ab_recv.at[slot])
    landed(nwin.at[pl.ds(0, 7)], nwin_recv)
    landed(gwin.at[pl.ds(0, 7)], gwin_recv)
    for copy in kept:
        copy.wait()
    tokens = (((0,), (0,)), ((), ()))
    both = ab[...].reshape(1024, 768)
    expanded = lax.dot_general(
        nwin[...].reshape(1024, 256), both[:, 384:], tokens, preferred_element_type=jnp.float32
    )
    odd = lax.rem(b, 2)
    reduced = lax.dot_general(
        gwin[...].reshape(1024, 256), both[:, :384], tokens, preferred_element_type=jnp.float32
    )

    @pl.when(odd == 0)
    def _():
        expand_ref[...] = expanded[:192]
        reduce_ref[...] = reduced[:192]

    @pl.when(odd == 1)
    def _():
        expand_ref[...] = expanded[64:]
        reduce_ref[...] = reduced[64:]

    @pl.when(holds_head)
    def _():
        @pl.loop(0, ROUNDS)
        def _(r):
            for copy in own_copies(r):
                copy.wait_send()
            for pair in relay_copies(r):
                for copy in pair:
                    copy.wait_send()
            opp_copy(r).wait_send()

        @pl.loop(1, ROUNDS)
        def _(r):
            wait_round(r)

        @pl.loop(0, 8)
        def _(n):
            @pl.when(jnp.logical_not(jnp.logical_and(n == b, z == home)))
            def _():
                o_copy(n).wait_send()

            @pl.when(n != b)
            def _():
                pool_copy(n).wait_send()

            @pl.when(jnp.logical_and(jnp.logical_and(home == 7, n < 7), n + 1 != b))
            def _():
                edge_copy(n).wait_send()

        @pl.loop(1, 8)
        def _(j):
            spread_copy(j).wait_send()

    @pl.loop(0, FINE_HEADS)
    def _(h):
        @pl.when(jnp.logical_not(is_self(h)))
        def _():
            q_copy(h).wait_send()

    @pl.when(not_last)
    def _():
        row_copy(1, following).wait_send()
        tok_copy().wait_send()

    @pl.when(not_first)
    def _():
        row_copy(0, preceding).wait_send()

    @pl.loop(1, 8)
    def _(j):
        count_copy(j).wait_send()
        wide_copy(gw, gw_send, gw_recv, j).wait_send()
        sum_copy(j).wait_send()
        window_copy(nbuf, nwin, nwin_send, nwin_recv, j).wait_send()
        window_copy(gw, gwin, gwin_send, gwin_recv, j).wait_send()

    @pl.loop(1, 4)
    def _(j):
        same_core(j).wait_send()

    share(b, 0).wait_send()
    for j in range(1, 4):
        share(lax.rem(b + 2 * j, 8), j).wait_send()


def whole_step(*arrays):
    rows = 128
    vmem = pl.BlockSpec(memory_space=pltpu.VMEM)
    hbm = pl.BlockSpec(memory_space=pl.ANY)
    dma = pltpu.SemaphoreType.DMA
    f32, bf16 = jnp.float32, jnp.bfloat16
    return pl.pallas_call(
        step_kernel,
        name="step",
        out_shape=(
            jax.ShapeDtypeStruct((rows, 1536), bf16),
            jax.ShapeDtypeStruct((192, 384), f32),
            jax.ShapeDtypeStruct((192, 384), f32),
        ),
        in_specs=[vmem] * 2 + [hbm] * 7,
        out_specs=(vmem,) * 3,
        scratch_shapes=[
            pltpu.VMEM((rows, 768), bf16),
            pltpu.VMEM((rows, 768), bf16),
            pltpu.VMEM((rows, 768), bf16),
            pltpu.VMEM((rows, 1536), bf16),
            pltpu.VMEM((8, rows, HEAD), bf16),
            pltpu.VMEM((ROUNDS, 2, 8, rows, HEAD), bf16),
            pltpu.VMEM((8, rows, 2 * HEAD), f32),
            pltpu.VMEM((8, rows, HEAD), f32),
            pltpu.VMEM((8, rows, HEAD), bf16),
            pltpu.VMEM((8, 32, HEAD), bf16),
            pltpu.VMEM((rows, 768), bf16),
            pltpu.VMEM((rows, 768), bf16),
            pltpu.VMEM((272, HEAD), bf16),
            pltpu.VMEM((rows, HEAD), bf16),
            pltpu.VMEM((768, 1536), bf16),
            pltpu.VMEM((1536, 384), bf16),
            pltpu.VMEM((384, 1536), bf16),
            pltpu.VMEM((24, 1536), f32),
            pltpu.VMEM((16, 1536), f32),
            pltpu.VMEM((24, 1536), f32),
            pltpu.VMEM((2, 1, 1536), f32),
            pltpu.VMEM((2, 1, 1536), f32),
            pltpu.VMEM((1, 128), jnp.int32),
            pltpu.VMEM((8, 16, 128), bf16),
            pltpu.VMEM((128, 1536), bf16),
            pltpu.VMEM((128, 1536), bf16),
            pltpu.VMEM((128, 1536), bf16),
            pltpu.VMEM((128, 1536), bf16),
            pltpu.VMEM((7, 16, 1536), bf16),
            pltpu.VMEM((8, 128, 768), bf16),
            pltpu.VMEM((8, 128, 256), bf16),
            pltpu.VMEM((8, 128, 256), bf16),
            pltpu.VMEM((128, 1536), f32),
            pltpu.SemaphoreType.REGULAR,
            dma((7,)),
            dma((FINE_HEADS,)),
            dma((ROUNDS, 2)),
            dma((ROUNDS, 3)),
            dma((ROUNDS, 4)),
            dma((ROUNDS,)),
            dma((8,)),
            dma((8,)),
            dma((8,)),
            dma((7,)),
            dma((8,)),
            dma((ROUNDS, 8)),
            dma,
            dma,
            dma,
            dma,
            dma((2,)),
            dma((2,)),
            dma,
            dma,
            dma((7,)),
            dma,
            dma((7,)),
            dma((7,)),
            dma((3,)),
            dma((4,)),
            dma((8,)),
            dma((8,)),
            dma,
            dma,
            dma((8,)),
            dma,
            dma,
        ],
        compiler_params=pltpu.CompilerParams(collective_id=0, has_side_effects=True),
    )(*arrays)


def local(
    token_ids,
    embedding,
    queries,
    key_rows,
    value_rows,
    head_mixer,
    expand_weight,
    reduce_weight,
    cotangent,
):
    restored, expand_grad, reduce_grad = whole_step(
        token_ids.reshape(1, -1),
        embedding,
        queries,
        key_rows,
        value_rows,
        cotangent,
        head_mixer,
        expand_weight,
        reduce_weight,
    )
    return restored, expand_grad, reduce_grad.T


def solution(mesh):
    return jax.shard_map(
        local,
        mesh=mesh,
        in_specs=(
            P(("dp", "blk", "wide")),
            P(),
            P(("dp", "blk", "wide"), None),
            P(("dp", "blk", "wide"), None),
            P(("dp", "blk", "wide"), None),
            P(),
            P(None, "wide"),
            P("wide", None),
            P(("dp", "blk", "wide"), None),
        ),
        out_specs=(
            P(("dp", "blk", "wide"), None),
            P(("dp", "blk"), "wide"),
            P(("dp", "wide"), "blk"),
        ),
        check_vma=False,
    )
```
